32 devices in a mesh: dom: 4 (over y, x), orb: 8 (over z, core).
Axes of the slice: x: 2, y: 2, z: 4, core: 2. Of those that a mesh axis runs over, the one named last changes fastest.
Arguments:
- orbitals: float32 [32, 32, 768], P('dom', 'orb'), may hold values from -24 to 24
- potential: float32 [32, 768], P('dom'), may hold values from -2 to 2
Outputs:
- gram_blocks: float32 [2, 32, 32], P(None, 'orb', 'dom')
The draws below stay inside these ranges and needn't reach their ends.
All inputs are finite; a program needn't handle non-finite values.
Results may differ from the reference program's by a relative error of at most 0.00005.
Values sent between devices are 32-bit elements; how exact they have to be, the bound alone decides.
No kernel may reach another device: no remote copies, remote signals or barrier semaphores. Data moves between devices by JAX's collectives and lax.ppermute only.
A program may use at most 64 MiB of HBM per device.

```python
import jax
import jax.numpy as jnp
from jax import lax

NZ = 96
NY = 8
ORB_DEV = 4
DEGREE = 2
NX = 32
ORBS = 32
PLANE = 768
CELLS = 24576


def draw_orbitals(key, part):
    keys = jax.random.split(key, 3)
    noise = jax.random.truncated_normal(keys[0], -4.0, 4.0, (NX, ORBS, PLANE), jnp.float32)
    fields = jax.random.truncated_normal(keys[1], -4.0, 4.0, (NX, 8, PLANE), jnp.float32)
    mixing = jax.random.uniform(keys[2], (ORBS, 8), jnp.float32, -0.9, 0.9)
    envelope = 1.0 + 2.0 * jnp.arange(NX, dtype=jnp.float32) / max(NX - 1, 1)
    common = jnp.einsum('ok,xkp->xop', mixing, fields) * envelope[:, None, None]
    return jnp.clip(noise + common, -24.0, 24.0)


def steps_of(stream_key, dims, cuts, least, high):
    loudness = 1.0
    for axis_at, shards_of in cuts:
        heights = jax.random.uniform(jax.random.fold_in(jax.random.fold_in(stream_key, 6), axis_at), (shards_of,), jnp.float32, least / len(cuts), high / len(cuts))
        loudness = loudness * jnp.repeat(jnp.exp(heights), dims[axis_at] // shards_of).reshape((-1,) + (1,) * (len(dims) - 1 - axis_at))
    return loudness


def setup_inputs(seed: int = 0) -> dict:
    seeds = jax.random.split(jax.random.key(seed), 3)
    return {
        "orbitals": draw_orbitals(jax.random.fold_in(seeds[2], 71), 0),
        "potential": jnp.clip(jax.random.uniform(seeds[1], (NX, PLANE), jnp.float32, -2.0, 2.0) * steps_of(seeds[1], (NX, PLANE), ((0, 4),), -0.4, 0.0), -2.0, 2.0),
    }


coeffs = (-5369.0 / 1800.0, 12.0 / 7.0, -15.0 / 56.0, 10.0 / 189.0, -1.0 / 112.0, 2.0 / 1925.0, -1.0 / 16632.0)
center_value = 6.5
half_value = 6.5


def hamiltonian(field, potential):
    planes = field.shape[0]
    count = field.shape[1]
    cube = field.reshape(planes, count, NY, NZ)
    lap = 3.0 * coeffs[0] * cube
    for step in range(1, 7):
        near = jnp.roll(cube, step, 0) + jnp.roll(cube, -step, 0)
        near = near + jnp.roll(cube, step, 2) + jnp.roll(cube, -step, 2)
        near = near + jnp.roll(cube, step, 3) + jnp.roll(cube, -step, 3)
        lap = lap + coeffs[step] * near
    return (-0.5 * lap).reshape(planes, count, NY * NZ) + potential[:, None, :] * field


def reference(orbitals, potential):
    groups = ORBS // ORB_DEV
    blocks = orbitals.reshape(NX, groups, ORB_DEV, PLANE).transpose(1, 0, 2, 3)

    def filtering(block):
        previous = block
        current = (hamiltonian(block, potential) - center_value * block) / half_value
        for step in range(DEGREE - 1):
            following = 2.0 * (hamiltonian(current, potential) - center_value * current) / half_value - previous
            previous = current
            current = following
        return current, hamiltonian(current, potential)

    filtered, applied = lax.map(filtering, blocks)
    filtered = filtered.transpose(0, 2, 1, 3).reshape(ORBS, NX * PLANE)
    applied = applied.transpose(0, 2, 1, 3).reshape(ORBS, NX * PLANE)
    correlation = jnp.dot(filtered, filtered.T, precision=lax.Precision.HIGHEST, preferred_element_type=jnp.float32) / CELLS
    projected = jnp.dot(filtered, applied.T, precision=lax.Precision.HIGHEST, preferred_element_type=jnp.float32) / CELLS
    return jnp.stack([correlation, projected])
```

```python
import functools

import jax
import jax.numpy as jnp
from jax import lax
from jax.experimental import pallas as pl
from jax.experimental.pallas import tpu as pltpu
from jax.sharding import PartitionSpec as P

NZ = 96
NY = 8
RADIUS = 6
LANES = 128


coeffs = (
    -5369.0 / 1800.0,
    12.0 / 7.0,
    -15.0 / 56.0,
    10.0 / 189.0,
    -1.0 / 112.0,
    2.0 / 1925.0,
    -1.0 / 16632.0,
)
center_value = 6.5
half_value = 6.5


def turned(tile, shift, axis=1):
    shift = shift % tile.shape[axis]
    return tile if shift == 0 else pltpu.roll(tile, shift, axis)


def wrapped(tile, lane):
    spare = (LANES - NZ) // 2
    after = turned(tile, NZ)
    before = turned(tile, LANES - NZ)
    return jnp.where(lane < NZ, tile, jnp.where(lane < NZ + spare, after, before))


def line_of(flat, row, lane):
    first, offset = divmod(row * NZ, LANES)
    line = turned(flat[:, first * LANES : (first + 1) * LANES], -offset)
    if offset + NZ > LANES:
        after = turned(flat[:, (first + 1) * LANES : (first + 2) * LANES], -offset)
        line = jnp.where(lane < LANES - offset, line, after)
    return wrapped(line, lane)


def stencil(load, at, scale):
    tile = load(at)
    rows = {s: turned(tile, s, 0) + turned(tile, -s, 0) for s in (1, 2, 3)}
    middle = turned(tile, 4, 0)
    rows[4] = middle + middle
    rows[5], rows[6] = rows[3], rows[2]
    total = None
    for step in range(1, RADIUS + 1):
        near = load(at + step) + load(at - step)
        near = near + (turned(tile, step) + turned(tile, -step))
        near = near + rows[step]
        term = (scale * coeffs[step]) * near
        total = term if total is None else total + term
    return total


def pack_kernel(orbitals_ref, potential_ref, out_ref):
    count = orbitals_ref.shape[1]
    for orb in range(count):
        out_ref[orb] = orbitals_ref[:, orb, :]
    out_ref[count] = potential_ref[...]


def filter_kernel(*refs):
    blocks, (out_ref, grid_ref, one_ref, two_ref, three_ref, four_ref, save_ref) = (
        refs[:-7],
        refs[-7:],
    )
    fields, planes, _ = blocks[0].shape
    count = fields - 1
    total = planes * len(blocks)
    lane = lax.broadcasted_iota(jnp.int32, (NY, LANES), 1)

    for index, block in enumerate(blocks):
        for q in range(fields):
            flat = block[q]
            for row in range(NY):
                line = line_of(flat, row, lane)
                if q == count:
                    line = (line - center_value - 1.5 * coeffs[0]) / half_value
                grid_ref[q, pl.ds(index * planes * NY + row, planes, stride=NY), :] = line

    def tile_of(ref):
        def load(at):
            return ref[pl.ds((at % total) * NY, NY), :]

        return load

    def level(at):
        return grid_ref[count, pl.ds((at % total) * NY, NY), :]

    small = -0.5 / half_value

    def one_orbital(orb, carry):
        start = tile_of(grid_ref.at[orb])
        one, two, three, four = (tile_of(r) for r in (one_ref, two_ref, three_ref, four_ref))

        def put(ref, at, value):
            ref[pl.ds((at % total) * NY, NY), :] = value

        for at in range(total):
            put(one_ref, at, stencil(start, at, small) + level(at) * start(at))
        for at in range(total):
            twice = level(at)
            value = stencil(one, at, 2.0 * small) + (twice + twice) * one(at) - start(at)
            put(two_ref, at, wrapped(value, lane))
        for at in range(total):
            put(three_ref, at, stencil(two, at, small) + level(at) * two(at))
        for at in range(-RADIUS, planes + RADIUS):
            twice = level(at)
            value = stencil(three, at, 2.0 * small) + (twice + twice) * three(at) - two(at)
            if 0 <= at < planes:
                value = wrapped(value, lane)
            put(four_ref, at, value)
        for at in range(planes):
            scaled = stencil(four, at, small) + level(at) * four(at)
            value = half_value * scaled + center_value * four(at)
            save_ref[count + orb, pl.ds(at * NY, NY), :] = value
            save_ref[orb, pl.ds(at * NY, NY), :] = four(at)
        return carry

    lax.fori_loop(0, count, one_orbital, 0)

    rows = 2 * count
    for at in range(planes):
        lines = [save_ref[:, at * NY + row, :] for row in range(NY)]
        for tile in range(NY * NZ // LANES):
            first = tile * LANES
            value = None
            for row in range(NY):
                low, high = max(row * NZ, first), min((row + 1) * NZ, first + LANES)
                if low >= high:
                    continue
                piece = turned(lines[row], row * NZ - first)
                value = piece if value is None else jnp.where(lane < low - first, value, piece)
            out_ref[pl.ds(at * rows, rows), first : first + LANES] = value


def gram_kernel(place_ref, *refs, planes, count, chips, total_cells):
    left_ref, units, out_ref = refs[0], refs[1:-1], refs[-1]
    rows = 2 * count
    cells = left_ref.shape[1]
    right = jnp.concatenate([u[...].reshape(planes * count, cells) for u in units], axis=0)
    full = lax.dot_general(
        left_ref[...],
        right,
        (((1,), (1,)), ((), ())),
        precision=lax.Precision.HIGHEST,
        preferred_element_type=jnp.float32,
    )
    width = full.shape[1]
    col = lax.broadcasted_iota(jnp.int32, (rows, width), 1)
    plane_of = (col % (planes * count)) // count
    total = None
    for at in range(planes):
        part = jnp.where(plane_of == at, full[at * rows : (at + 1) * rows], 0.0)
        total = part if total is None else total + part
    total = total * (1.0 / total_cells)
    half = width // 2
    halves = []
    for index in range(2):
        part = total[:, index * half : (index + 1) * half]
        step = count
        while step < planes * count:
            part = part + turned(part, -step)
            step *= 2
        halves.append(part)
    chip, core, dom = place_ref[0], place_ref[1], place_ref[2]
    even = jnp.where(core == 0, halves[0], halves[1])
    odd = jnp.where(core == 0, halves[1], halves[0])
    lane = lax.broadcasted_iota(jnp.int32, (rows, half), 1) % (planes * count)
    joined = jnp.where(lane < count, even, turned(odd, count))
    for flip in range(chips):
        target = lax.rem((chip ^ flip) - dom + chips, chips)
        out_ref[target] = turned(joined, -flip * planes * count)[:, :LANES]


def sum_kernel(*refs):
    parts, out_ref = refs[:-1], refs[-1]
    total = parts[0][...]
    for part in parts[1:]:
        total = total + part[...]
    first, rows, columns = out_ref.shape
    for index in range(first):
        out_ref[index] = total[index * rows : (index + 1) * rows, :columns]


VMEM = pl.BlockSpec(memory_space=pltpu.VMEM)
SMEM = pl.BlockSpec(memory_space=pltpu.SMEM)


def gathered_device(orbitals, potential):
    doms, orbs = lax.axis_size("dom"), lax.axis_size("orb")
    chips = orbs // 2
    planes, count, cells = orbitals.shape
    total = planes * doms

    def swap_orb(value, flip):
        return lax.ppermute(value, "orb", [(i, i ^ flip) for i in range(orbs)])

    def from_next(value, step):
        return lax.ppermute(value, "dom", [((i + step) % doms, i) for i in range(doms)])

    flips = list(range(1, chips))
    flips.sort(key=lambda f: -f)
    near = {0: orbitals}
    for flip in flips:
        near[flip] = swap_orb(orbitals, 2 * flip)

    packed = pl.pallas_call(
        pack_kernel,
        out_shape=jax.ShapeDtypeStruct((count + 1, planes, cells), jnp.float32),
        in_specs=[VMEM, VMEM],
        out_specs=VMEM,
        name="pack",
    )(orbitals, potential)
    blocks = [packed] + [from_next(packed, step) for step in range(1, doms)]

    far = {flip: swap_orb(near[flip], 1) for flip in range(chips)}

    apps = count * (3 * total + 2 * planes + 2 * RADIUS)
    left = pl.pallas_call(
        filter_kernel,
        out_shape=jax.ShapeDtypeStruct((planes * 2 * count, cells), jnp.float32),
        in_specs=[VMEM] * doms,
        out_specs=VMEM,
        scratch_shapes=[pltpu.VMEM((count + 1, total * NY, LANES), jnp.float32)]
        + [pltpu.VMEM((total * NY, LANES), jnp.float32)] * 4
        + [pltpu.VMEM((2 * count, planes * NY, LANES), jnp.float32)],
        cost_estimate=pl.CostEstimate(
            flops=apps * NY * LANES * 50, bytes_accessed=(count + 1) * total * cells * 4, transcendentals=0
        ),
        name="filter",
    )(*blocks)

    here = lax.axis_index("orb")
    place = jnp.stack([here // 2, here % 2, lax.axis_index("dom")]).astype(jnp.int32)
    units = [near[flip] for flip in range(chips)] + [far[flip] for flip in range(chips)]
    shares = pl.pallas_call(
        functools.partial(
            gram_kernel, planes=planes, count=count, chips=chips, total_cells=total * cells
        ),
        out_shape=jax.ShapeDtypeStruct((doms, 2 * count, LANES), jnp.float32),
        in_specs=[SMEM] + [VMEM] * (1 + len(units)),
        out_specs=VMEM,
        name="gram",
    )(place, left, *units)
    parts = [shares[0]] + [
        lax.ppermute(shares[k], "dom", [(i, (i + k) % doms) for i in range(doms)])
        for k in range(1, doms)
    ]
    return pl.pallas_call(
        sum_kernel,
        out_shape=jax.ShapeDtypeStruct((2, count, orbs * count // doms), jnp.float32),
        in_specs=[VMEM] * doms,
        out_specs=VMEM,
        name="total",
    )(*parts)


def with_halo(cells, sides, width):
    for axis, dim in sides:
        count = lax.axis_size(axis)
        head = lax.slice_in_dim(cells, 0, width, axis=dim)
        tail = lax.slice_in_dim(cells, cells.shape[dim] - width, cells.shape[dim], axis=dim)
        cells = jnp.concatenate(
            [
                lax.ppermute(tail, axis, [(i, (i + 1) % count) for i in range(count)]),
                cells,
                lax.ppermute(head, axis, [((i + 1) % count, i) for i in range(count)]),
            ],
            axis=dim,
        )
    return cells


def periodic_pad(cube, axis_index):
    extent = cube.shape[axis_index]
    lower = lax.slice_in_dim(cube, extent - RADIUS, extent, axis=axis_index)
    upper = lax.slice_in_dim(cube, 0, RADIUS, axis=axis_index)
    return jnp.concatenate([lower, cube, upper], axis=axis_index)


def stencil_apply(padded, potential, count):
    offset = (potential.shape[0] - count) // 2
    middle = padded[RADIUS : RADIUS + count]
    width = middle.shape[1]
    cube = middle.reshape(count, width, NY, NZ)
    y_padded = periodic_pad(cube, 2)
    z_padded = periodic_pad(cube, 3)
    lap = 3.0 * coeffs[0] * cube
    for step in range(1, 7):
        near = (
            padded[RADIUS + step : RADIUS + step + count]
            + padded[RADIUS - step : RADIUS - step + count]
        )
        near = near.reshape(count, width, NY, NZ)
        near = (
            near
            + y_padded[:, :, RADIUS - step : RADIUS - step + NY]
            + y_padded[:, :, RADIUS + step : RADIUS + step + NY]
        )
        near = (
            near
            + z_padded[:, :, :, RADIUS - step : RADIUS - step + NZ]
            + z_padded[:, :, :, RADIUS + step : RADIUS + step + NZ]
        )
        lap = lap + coeffs[step] * near
    return (-0.5 * lap).reshape(count, width, NY * NZ) + potential[
        offset : offset + count, None, :
    ] * middle


def apply_field(field, potential):
    padded = with_halo(field, (("dom", 0),), RADIUS)
    return stencil_apply(padded, potential, field.shape[0])


def on_device(orbitals, potential):
    planes = orbitals.shape[0]
    current = (apply_field(orbitals, potential) - center_value * orbitals) / half_value
    following = (
        2.0 * (apply_field(current, potential) - center_value * current) / half_value - orbitals
    )
    applied = apply_field(following, potential)
    filt_cells, appl_cells = (
        lax.all_to_all(following, "orb", split_axis=2, concat_axis=1, tiled=True),
        lax.all_to_all(applied, "orb", split_axis=2, concat_axis=1, tiled=True),
    )
    total_cells = planes * lax.axis_size("dom") * orbitals.shape[2]
    correlation = jnp.einsum(
        "xop,xqp->oq",
        filt_cells,
        filt_cells,
        precision=lax.Precision.HIGHEST,
        preferred_element_type=jnp.float32,
    )
    projected = jnp.einsum(
        "xop,xqp->oq",
        filt_cells,
        appl_cells,
        precision=lax.Precision.HIGHEST,
        preferred_element_type=jnp.float32,
    )
    partial_blocks = jnp.stack([correlation, projected]) / total_cells
    row_blocks = lax.psum_scatter(partial_blocks, "orb", scatter_dimension=1, tiled=True)
    return lax.psum_scatter(row_blocks, "dom", scatter_dimension=2, tiled=True)


def fits_gather(mesh):
    doms, orbs = mesh.shape["dom"], mesh.shape["orb"]
    return orbs == 2 * doms and doms <= 4 and doms & (doms - 1) == 0


def solution(mesh):
    return jax.shard_map(
        gathered_device if fits_gather(mesh) else on_device,
        mesh=mesh,
        in_specs=(P("dom", "orb", None), P("dom", None)),
        out_specs=P(None, "orb", "dom"),
        check_vma=False,
    )
```

```python
import functools

import jax
import jax.numpy as jnp
import numpy as np
from jax import lax
from jax.experimental import pallas as pl
from jax.experimental.pallas import tpu as pltpu
from jax.sharding import PartitionSpec as P

NZ = 96
NY = 8
RADIUS = 6
LANES = 128


coeffs = (
    -5369.0 / 1800.0,
    12.0 / 7.0,
    -15.0 / 56.0,
    10.0 / 189.0,
    -1.0 / 112.0,
    2.0 / 1925.0,
    -1.0 / 16632.0,
)
center_value = 6.5
half_value = 6.5


def turned(tile, shift, axis=1):
    shift = shift % tile.shape[axis]
    return tile if shift == 0 else pltpu.roll(tile, shift, axis)


def line_of(flat, row, lane):
    first, offset = divmod(row * NZ, LANES)
    line = turned(flat[:, first * LANES : (first + 1) * LANES], -offset)
    if offset + NZ > LANES:
        after = turned(flat[:, (first + 1) * LANES : (first + 2) * LANES], -offset)
        line = jnp.where(lane < LANES - offset, line, after)
    return jnp.where(lane < NZ, line, 0.0)


Z_FACTOR = 1.09375


def z_matrix():
    matrix = np.zeros((LANES, LANES), np.float64)
    for cell in range(NZ):
        for step in range(1, RADIUS + 1):
            matrix[cell, (cell + step) % NZ] += coeffs[step] * Z_FACTOR
            matrix[cell, (cell - step) % NZ] += coeffs[step] * Z_FACTOR
    leading = matrix.astype(jnp.bfloat16)
    trailing = (matrix - leading.astype(np.float64)).astype(jnp.bfloat16)
    both = np.concatenate([leading, trailing], axis=1)
    return np.concatenate([both, both], axis=0)


def stencil(load, at, along_z, scale):
    tile = load(at)
    rows = {s: turned(tile, s, 0) + turned(tile, -s, 0) for s in (1, 2, 3)}
    middle = turned(tile, 4, 0)
    rows[4] = middle + middle
    rows[5], rows[6] = rows[3], rows[2]
    total = (scale / Z_FACTOR) * along_z
    for step in range(1, RADIUS + 1):
        near = load(at + step) + load(at - step) + rows[step]
        total = total + (scale * coeffs[step]) * near
    return total


def pack_kernel(orbitals_ref, potential_ref, out_ref):
    count = orbitals_ref.shape[1]
    for orb in range(count):
        out_ref[orb] = orbitals_ref[:, orb, :]
    out_ref[count] = potential_ref[...]


def filter_kernel(matrix_ref, *refs):
    blocks, refs = refs[:-8], refs[-8:]
    out_ref, grid_ref, one_ref, two_ref, three_ref, four_ref, z_ref, save_ref = refs
    fields, planes, _ = blocks[0].shape
    count = fields - 1
    total = planes * len(blocks)
    lane = lax.broadcasted_iota(jnp.int32, (NY, LANES), 1)

    for index, block in enumerate(blocks):
        for q in range(fields):
            flat = block[q]
            for row in range(NY):
                line = line_of(flat, row, lane)
                if q == count:
                    line = (line - center_value - 1.5 * coeffs[0]) / half_value
                grid_ref[q, pl.ds(index * planes * NY + row, planes, stride=NY), :] = line

    def tile_of(ref):
        def load(at):
            return ref[pl.ds((at % total) * NY, NY), :]

        return load

    def level(at):
        return grid_ref[count, pl.ds((at % total) * NY, NY), :]

    def z_pass(ref, first, number):
        cells = pl.ds(first * NY, number * NY)
        value = ref[cells, :]
        upper = value.astype(jnp.bfloat16)
        lower = (value - upper.astype(jnp.float32)).astype(jnp.bfloat16)
        product = jnp.dot(
            jnp.concatenate([upper, lower], axis=1),
            matrix_ref[...],
            preferred_element_type=jnp.float32,
        )
        z_ref[cells, :] = product[:, :LANES] + product[:, LANES:]

    small = -0.5 / half_value

    def one_orbital(orb, carry):
        start = tile_of(grid_ref.at[orb])
        one, two, three, four = (tile_of(r) for r in (one_ref, two_ref, three_ref, four_ref))
        along_z = tile_of(z_ref)

        def put(ref, at, value):
            ref[pl.ds((at % total) * NY, NY), :] = value

        z_pass(grid_ref.at[orb], 0, total)
        for at in range(total):
            put(one_ref, at, stencil(start, at, along_z(at), small) + level(at) * start(at))
        z_pass(one_ref, 0, total)
        for at in range(total):
            twice = level(at) + level(at)
            value = stencil(one, at, along_z(at), 2.0 * small) + twice * one(at)
            put(two_ref, at, value - start(at))
        z_pass(two_ref, 0, total)
        for at in range(total):
            put(three_ref, at, stencil(two, at, along_z(at), small) + level(at) * two(at))
        z_pass(three_ref, 0, planes + RADIUS)
        z_pass(three_ref, total - RADIUS, RADIUS)
        for at in range(-RADIUS, planes + RADIUS):
            twice = level(at) + level(at)
            value = stencil(three, at, along_z(at), 2.0 * small) + twice * three(at)
            put(four_ref, at, value - two(at))
        z_pass(four_ref, 0, planes)
        for at in range(planes):
            scaled = stencil(four, at, along_z(at), small) + level(at) * four(at)
            save_ref[orb, pl.ds(at * NY, NY), :] = four(at)
            save_ref[count + orb, pl.ds(at * NY, NY), :] = (
                half_value * scaled + center_value * four(at)
            )
        return carry

    lax.fori_loop(0, count, one_orbital, 0)

    rows = 2 * count
    for at in range(planes):
        lines = [save_ref[:, at * NY + row, :] for row in range(NY)]
        for tile in range(NY * NZ // LANES):
            first = tile * LANES
            value = None
            for row in range(NY):
                low, high = max(row * NZ, first), min((row + 1) * NZ, first + LANES)
                if low >= high:
                    continue
                piece = turned(lines[row], row * NZ - first)
                value = piece if value is None else jnp.where(lane < low - first, value, piece)
            out_ref[pl.ds(at * rows, rows), first : first + LANES] = value


def gram_kernel(place_ref, *refs, planes, count, chips, total_cells):
    left_ref, units, out_ref = refs[0], refs[1:-1], refs[-1]
    rows = 2 * count
    cells = left_ref.shape[1]
    right = jnp.concatenate([u[...].reshape(planes * count, cells) for u in units], axis=0)
    full = lax.dot_general(
        left_ref[...],
        right,
        (((1,), (1,)), ((), ())),
        precision=lax.Precision.HIGHEST,
        preferred_element_type=jnp.float32,
    )
    width = full.shape[1]
    col = lax.broadcasted_iota(jnp.int32, (rows, width), 1)
    plane_of = (col % (planes * count)) // count
    total = None
    for at in range(planes):
        part = jnp.where(plane_of == at, full[at * rows : (at + 1) * rows], 0.0)
        total = part if total is None else total + part
    total = total * (1.0 / total_cells)
    half = width // 2
    halves = []
    for index in range(2):
        part = total[:, index * half : (index + 1) * half]
        step = count
        while step < planes * count:
            part = part + turned(part, -step)
            step *= 2
        halves.append(part)
    chip, core, dom = place_ref[0], place_ref[1], place_ref[2]
    even = jnp.where(core == 0, halves[0], halves[1])
    odd = jnp.where(core == 0, halves[1], halves[0])
    lane = lax.broadcasted_iota(jnp.int32, (rows, half), 1) % (planes * count)
    joined = jnp.where(lane < count, even, turned(odd, count))
    for flip in range(chips):
        target = lax.rem((chip ^ flip) - dom + chips, chips)
        out_ref[target] = turned(joined, -flip * planes * count)[:, :LANES]


def sum_kernel(*refs):
    parts, out_ref = refs[:-1], refs[-1]
    total = parts[0][...]
    for part in parts[1:]:
        total = total + part[...]
    first, rows, columns = out_ref.shape
    for index in range(first):
        out_ref[index] = total[index * rows : (index + 1) * rows, :columns]


VMEM = pl.BlockSpec(memory_space=pltpu.VMEM)
SMEM = pl.BlockSpec(memory_space=pltpu.SMEM)
SMALL = pltpu.CompilerParams(vmem_limit_bytes=8 << 20)


def gathered_device(orbitals, potential):
    doms, orbs = lax.axis_size("dom"), lax.axis_size("orb")
    chips = orbs // 2
    planes, count, cells = orbitals.shape
    total = planes * doms

    def swap_orb(value, flip):
        return lax.ppermute(value, "orb", [(i, i ^ flip) for i in range(orbs)])

    def from_next(value, step):
        return lax.ppermute(value, "dom", [((i + step) % doms, i) for i in range(doms)])

    flips = list(range(1, chips))
    flips.sort(key=lambda f: -f)
    near = {0: orbitals}
    for flip in flips:
        near[flip] = swap_orb(orbitals, 2 * flip)

    packed = pl.pallas_call(
        pack_kernel,
        out_shape=jax.ShapeDtypeStruct((count + 1, planes, cells), jnp.float32),
        in_specs=[VMEM, VMEM],
        out_specs=VMEM,
        compiler_params=SMALL,
        name="pack",
    )(orbitals, potential)
    blocks = [packed] + [from_next(packed, step) for step in range(1, doms)]

    far = {flip: swap_orb(near[flip], 1) for flip in range(chips)}

    apps = count * (3 * total + 2 * planes + 2 * RADIUS)
    left = pl.pallas_call(
        filter_kernel,
        out_shape=jax.ShapeDtypeStruct((planes * 2 * count, cells), jnp.float32),
        in_specs=[VMEM] * (1 + doms),
        out_specs=VMEM,
        scratch_shapes=[pltpu.VMEM((count + 1, total * NY, LANES), jnp.float32)]
        + [pltpu.VMEM((total * NY, LANES), jnp.float32)] * 5
        + [pltpu.VMEM((2 * count, planes * NY, LANES), jnp.float32)],
        cost_estimate=pl.CostEstimate(
            flops=apps * NY * LANES * 50, bytes_accessed=(count + 1) * total * cells * 4, transcendentals=0
        ),
        compiler_params=SMALL,
        name="filter",
    )(jnp.asarray(z_matrix()), *blocks)

    here = lax.axis_index("orb")
    place = jnp.stack([here // 2, here % 2, lax.axis_index("dom")]).astype(jnp.int32)
    units = [near[flip] for flip in range(chips)] + [far[flip] for flip in range(chips)]
    shares = pl.pallas_call(
        functools.partial(
            gram_kernel, planes=planes, count=count, chips=chips, total_cells=total * cells
        ),
        out_shape=jax.ShapeDtypeStruct((doms, 2 * count, LANES), jnp.float32),
        in_specs=[SMEM] + [VMEM] * (1 + len(units)),
        out_specs=VMEM,
        compiler_params=SMALL,
        name="gram",
    )(place, left, *units)
    parts = [shares[0]] + [
        lax.ppermute(shares[k], "dom", [(i, (i + k) % doms) for i in range(doms)])
        for k in range(1, doms)
    ]
    return pl.pallas_call(
        sum_kernel,
        out_shape=jax.ShapeDtypeStruct((2, count, orbs * count // doms), jnp.float32),
        in_specs=[VMEM] * doms,
        out_specs=VMEM,
        compiler_params=SMALL,
        name="total",
    )(*parts)


def with_halo(cells, sides, width):
    for axis, dim in sides:
        count = lax.axis_size(axis)
        head = lax.slice_in_dim(cells, 0, width, axis=dim)
        tail = lax.slice_in_dim(cells, cells.shape[dim] - width, cells.shape[dim], axis=dim)
        cells = jnp.concatenate(
            [
                lax.ppermute(tail, axis, [(i, (i + 1) % count) for i in range(count)]),
                cells,
                lax.ppermute(head, axis, [((i + 1) % count, i) for i in range(count)]),
            ],
            axis=dim,
        )
    return cells


def periodic_pad(cube, axis_index):
    extent = cube.shape[axis_index]
    lower = lax.slice_in_dim(cube, extent - RADIUS, extent, axis=axis_index)
    upper = lax.slice_in_dim(cube, 0, RADIUS, axis=axis_index)
    return jnp.concatenate([lower, cube, upper], axis=axis_index)


def stencil_apply(padded, potential, count):
    offset = (potential.shape[0] - count) // 2
    middle = padded[RADIUS : RADIUS + count]
    width = middle.shape[1]
    cube = middle.reshape(count, width, NY, NZ)
    y_padded = periodic_pad(cube, 2)
    z_padded = periodic_pad(cube, 3)
    lap = 3.0 * coeffs[0] * cube
    for step in range(1, 7):
        near = (
            padded[RADIUS + step : RADIUS + step + count]
            + padded[RADIUS - step : RADIUS - step + count]
        )
        near = near.reshape(count, width, NY, NZ)
        near = (
            near
            + y_padded[:, :, RADIUS - step : RADIUS - step + NY]
            + y_padded[:, :, RADIUS + step : RADIUS + step + NY]
        )
        near = (
            near
            + z_padded[:, :, :, RADIUS - step : RADIUS - step + NZ]
            + z_padded[:, :, :, RADIUS + step : RADIUS + step + NZ]
        )
        lap = lap + coeffs[step] * near
    return (-0.5 * lap).reshape(count, width, NY * NZ) + potential[
        offset : offset + count, None, :
    ] * middle


def apply_field(field, potential):
    padded = with_halo(field, (("dom", 0),), RADIUS)
    return stencil_apply(padded, potential, field.shape[0])


def on_device(orbitals, potential):
    planes = orbitals.shape[0]
    current = (apply_field(orbitals, potential) - center_value * orbitals) / half_value
    following = (
        2.0 * (apply_field(current, potential) - center_value * current) / half_value - orbitals
    )
    applied = apply_field(following, potential)
    filt_cells, appl_cells = (
        lax.all_to_all(following, "orb", split_axis=2, concat_axis=1, tiled=True),
        lax.all_to_all(applied, "orb", split_axis=2, concat_axis=1, tiled=True),
    )
    total_cells = planes * lax.axis_size("dom") * orbitals.shape[2]
    correlation = jnp.einsum(
        "xop,xqp->oq",
        filt_cells,
        filt_cells,
        precision=lax.Precision.HIGHEST,
        preferred_element_type=jnp.float32,
    )
    projected = jnp.einsum(
        "xop,xqp->oq",
        filt_cells,
        appl_cells,
        precision=lax.Precision.HIGHEST,
        preferred_element_type=jnp.float32,
    )
    partial_blocks = jnp.stack([correlation, projected]) / total_cells
    row_blocks = lax.psum_scatter(partial_blocks, "orb", scatter_dimension=1, tiled=True)
    return lax.psum_scatter(row_blocks, "dom", scatter_dimension=2, tiled=True)


def fits_gather(mesh):
    doms, orbs = mesh.shape["dom"], mesh.shape["orb"]
    return orbs == 2 * doms and doms <= 4 and doms & (doms - 1) == 0


def solution(mesh):
    return jax.shard_map(
        gathered_device if fits_gather(mesh) else on_device,
        mesh=mesh,
        in_specs=(P("dom", "orb", None), P("dom", None)),
        out_specs=P(None, "orb", "dom"),
        check_vma=False,
    )
```

```python
import functools

import jax
import jax.numpy as jnp
import numpy as np
from jax import lax
from jax.experimental import pallas as pl
from jax.experimental.pallas import tpu as pltpu
from jax.sharding import PartitionSpec as P


NZ = 96
NY = 8
RADIUS = 6
LANES = 128


coeffs = (
    -5369.0 / 1800.0,
    12.0 / 7.0,
    -15.0 / 56.0,
    10.0 / 189.0,
    -1.0 / 112.0,
    2.0 / 1925.0,
    -1.0 / 16632.0,
)
center_value = 6.5
half_value = 6.5


def turned(tile, shift, axis=1):
    shift = shift % tile.shape[axis]
    return tile if shift == 0 else pltpu.roll(tile, shift, axis)


def line_of(flat, row, lane):
    first, offset = divmod(row * NZ, LANES)
    line = turned(flat[:, first * LANES : (first + 1) * LANES], -offset)
    if offset + NZ > LANES:
        after = turned(flat[:, (first + 1) * LANES : (first + 2) * LANES], -offset)
        line = jnp.where(lane < LANES - offset, line, after)
    return jnp.where(lane < NZ, line, 0.0)


Z_FACTOR = 1.09375


def z_matrix():
    matrix = np.zeros((LANES, LANES), np.float64)
    for cell in range(NZ):
        for step in range(1, RADIUS + 1):
            matrix[cell, (cell + step) % NZ] += coeffs[step] * Z_FACTOR
            matrix[cell, (cell - step) % NZ] += coeffs[step] * Z_FACTOR
    leading = matrix.astype(jnp.bfloat16)
    trailing = (matrix - leading.astype(np.float64)).astype(jnp.bfloat16)
    both = np.concatenate([leading, trailing], axis=1)
    return np.concatenate([both, both], axis=0)


def stencil(load, at, along_z, scale):
    tile = load(at)
    rows = {s: turned(tile, s, 0) + turned(tile, -s, 0) for s in (1, 2, 3)}
    middle = turned(tile, 4, 0)
    rows[4] = middle + middle
    rows[5], rows[6] = rows[3], rows[2]
    total = (scale / Z_FACTOR) * along_z
    for step in range(1, RADIUS + 1):
        near = load(at + step) + load(at - step) + rows[step]
        total = total + (scale * coeffs[step]) * near
    return total


def pack_kernel(orbitals_ref, potential_ref, out_ref, held_ref, sems):
    planes, count, cells = orbitals_ref.shape
    field = pltpu.make_async_copy(orbitals_ref, out_ref.at[pl.ds(0, planes)], sems.at[0])
    level = pltpu.make_async_copy(potential_ref, held_ref, sems.at[1])
    level.start()
    field.start()
    level.wait()
    out_ref[pl.ds(planes, planes // count)] = held_ref[...].reshape(planes // count, count, cells)
    field.wait()


def filter_kernel(matrix_ref, *refs):
    blocks, refs = refs[:-8], refs[-8:]
    out_ref, grid_ref, one_ref, two_ref, three_ref, four_ref, z_ref, save_ref = refs
    count, planes = blocks[0].shape[1], out_ref.shape[0] // (2 * blocks[0].shape[1])
    total = planes * len(blocks)
    lane = lax.broadcasted_iota(jnp.int32, (NY, LANES), 1)

    dom = lax.axis_index("dom")
    for index, block in enumerate(blocks):
        place = pl.multiple_of((((dom ^ index) - dom) & (len(blocks) - 1)) * planes * NY, planes * NY)
        for q in range(count + 1):
            if q < count:
                flat = block[pl.ds(0, planes), q, :]
            else:
                flat = block[pl.ds(planes, planes // count)].reshape(planes, block.shape[2])
            for row in range(NY):
                line = line_of(flat, row, lane)
                if q == count:
                    line = (line - center_value - 1.5 * coeffs[0]) / half_value
                grid_ref[q, pl.ds(place + row, planes, stride=NY), :] = line

    def tile_of(ref):
        def load(at):
            return ref[pl.ds((at % total) * NY, NY), :]

        return load

    def level(at):
        return grid_ref[count, pl.ds((at % total) * NY, NY), :]

    def z_pass(ref, first, number):
        cells = pl.ds(first * NY, number * NY)
        value = ref[cells, :]
        upper = value.astype(jnp.bfloat16)
        lower = (value - upper.astype(jnp.float32)).astype(jnp.bfloat16)
        product = jnp.dot(
            jnp.concatenate([upper, lower], axis=1),
            matrix_ref[...],
            preferred_element_type=jnp.float32,
        )
        z_ref[cells, :] = product[:, :LANES] + product[:, LANES:]

    small = -0.5 / half_value

    def one_orbital(orb, carry):
        start = tile_of(grid_ref.at[orb])
        one, two, three, four = (tile_of(r) for r in (one_ref, two_ref, three_ref, four_ref))
        along_z = tile_of(z_ref)

        def put(ref, at, value):
            ref[pl.ds((at % total) * NY, NY), :] = value

        z_pass(grid_ref.at[orb], 0, total)
        for at in range(total):
            put(one_ref, at, stencil(start, at, along_z(at), small) + level(at) * start(at))
        z_pass(one_ref, 0, total)
        for at in range(total):
            twice = level(at) + level(at)
            value = stencil(one, at, along_z(at), 2.0 * small) + twice * one(at)
            put(two_ref, at, value - start(at))
        z_pass(two_ref, 0, total)
        for at in range(total):
            put(three_ref, at, stencil(two, at, along_z(at), small) + level(at) * two(at))
        z_pass(three_ref, 0, planes + RADIUS)
        z_pass(three_ref, total - RADIUS, RADIUS)
        for at in range(-RADIUS, planes + RADIUS):
            twice = level(at) + level(at)
            value = stencil(three, at, along_z(at), 2.0 * small) + twice * three(at)
            put(four_ref, at, value - two(at))
        z_pass(four_ref, 0, planes)
        for at in range(planes):
            scaled = stencil(four, at, along_z(at), small) + level(at) * four(at)
            save_ref[orb, pl.ds(at * NY, NY), :] = four(at)
            save_ref[count + orb, pl.ds(at * NY, NY), :] = (
                half_value * scaled + center_value * four(at)
            )
        return carry

    lax.fori_loop(0, count, one_orbital, 0)

    rows = 2 * count
    for at in range(planes):
        lines = [save_ref[:, at * NY + row, :] for row in range(NY)]
        for tile in range(NY * NZ // LANES):
            first = tile * LANES
            value = None
            for row in range(NY):
                low, high = max(row * NZ, first), min((row + 1) * NZ, first + LANES)
                if low >= high:
                    continue
                piece = turned(lines[row], row * NZ - first)
                value = piece if value is None else jnp.where(lane < low - first, value, piece)
            out_ref[pl.ds(at * rows, rows), first : first + LANES] = value


def split(value):
    upper = value.astype(jnp.bfloat16)
    lower = (value - upper.astype(jnp.float32)).astype(jnp.bfloat16)
    return upper, lower


def products(left, units, planes, count):
    upper, lower = split(left)
    cells = left.shape[1]
    lines = [
        jnp.zeros((planes * count, cells), jnp.float32)
        if unit is None
        else unit[pl.ds(0, planes)].reshape(planes * count, cells)
        for unit in units
    ]
    right_upper, right_lower = split(jnp.concatenate(lines, axis=0))

    def product(one, two):
        return lax.dot_general(
            one, two, (((1,), (1,)), ((), ())), preferred_element_type=jnp.float32
        )

    number = left.shape[0]
    full = product(jnp.concatenate([upper, lower], axis=0), right_upper)
    full = full[:number] + (full[number:] + product(upper, right_lower))
    rows = 2 * count
    plane_of = lax.broadcasted_iota(jnp.int32, (rows, full.shape[1]), 1)
    plane_of = (plane_of % (planes * count)) // count
    total = None
    for at in range(planes):
        part = jnp.where(plane_of == at, full[at * rows : (at + 1) * rows], 0.0)
        total = part if total is None else total + part
    return total


def early_kernel(left_ref, *refs, planes, count):
    units, out_ref = refs[:-1], refs[-1]
    half = len(units) // 2
    listed = (*units[:half], None, *units[half:], None)
    out_ref[...] = products(left_ref[...], listed, planes, count)


def late_kernel(left_ref, early_ref, near_ref, far_ref, out_ref, *, planes, count, flips, total_cells):
    line = planes * count
    late = products(left_ref[...], (near_ref, far_ref), planes, count) * (1.0 / total_cells)
    early = early_ref[...] * (1.0 / total_cells)
    width = early.shape[1] // 2
    rows = late.shape[0]
    lane = lax.broadcasted_iota(jnp.int32, (rows, width), 1)
    late = jnp.concatenate([late, jnp.zeros((rows, width - 2 * line), jnp.float32)], axis=1)
    halves = []
    for index in range(2):
        moved = turned(late, width - (1 + index) * line)
        part = early[:, index * width : (index + 1) * width]
        part = jnp.where(lane < width - line, part, moved)
        step = count
        while step < line:
            part = part + turned(part, -step)
            step *= 2
        halves.append(part)
    dom, orb = lax.axis_index("dom"), lax.axis_index("orb")
    chip, core = orb >> 1, orb & 1
    even = jnp.where(core == 0, halves[0], halves[1])
    odd = jnp.where(core == 0, halves[1], halves[0])
    joined = jnp.where(lane % line < count, even, turned(odd, count))
    for slot, flip in enumerate(flips):
        out_ref[chip ^ flip ^ dom] = turned(joined, -slot * line)


def sum_kernel(*refs):
    parts, out_ref = refs[:-1], refs[-1]
    total = parts[0][...]
    for part in parts[1:]:
        total = total + part[...]
    first, rows, columns = out_ref.shape
    for index in range(first):
        out_ref[index] = total[index * rows : (index + 1) * rows, :columns]


VMEM = pl.BlockSpec(memory_space=pltpu.VMEM)
HBM = pl.BlockSpec(memory_space=pltpu.HBM)
SMALL = pltpu.CompilerParams(vmem_limit_bytes=8 << 20)


def gathered_device(orbitals, potential):
    return gathered_steps(orbitals, potential)


def gathered_steps(orbitals, potential):
    doms, orbs = lax.axis_size("dom"), lax.axis_size("orb")
    chips = orbs // 2
    planes, count, cells = orbitals.shape
    total = planes * doms

    def swap_orb(value, flip):
        return lax.ppermute(value, "orb", [(i, i ^ flip) for i in range(orbs)])

    def along_dom(value, step):
        return lax.ppermute(value, "dom", [(i, i ^ step) for i in range(doms)])

    packed = pl.pallas_call(
        pack_kernel,
        out_shape=jax.ShapeDtypeStruct((planes + planes // count, count, cells), jnp.float32),
        in_specs=[HBM, HBM],
        out_specs=VMEM,
        scratch_shapes=[pltpu.VMEM((planes, cells), jnp.float32), pltpu.SemaphoreType.DMA((2,))],
        compiler_params=SMALL,
        name="pack",
    )(
        pltpu.with_memory_space_constraint(orbitals, pltpu.HBM),
        pltpu.with_memory_space_constraint(potential, pltpu.HBM),
    )
    others = {step: along_dom(packed, step) for step in range(1, doms)}
    blocks = [packed] + [others[step] for step in range(1, doms)]

    flips = (0, *FLIPS) if chips == 1 + len(FLIPS) else tuple(range(chips))
    near = {0: packed}
    for flip in flips[1:]:
        near[flip] = swap_orb(orbitals, 2 * flip)
    far = {0: swap_orb(orbitals, 1)}
    for flip in flips[1:]:
        if flip == CROSS:
            far[flip] = swap_orb(orbitals, 2 * flip + 1)
        else:
            far[flip] = swap_orb(near[flip], 1)

    apps = count * (3 * total + 2 * planes + 2 * RADIUS)
    left = pl.pallas_call(
        filter_kernel,
        out_shape=jax.ShapeDtypeStruct((planes * 2 * count, cells), jnp.float32),
        in_specs=[VMEM] * (1 + doms),
        out_specs=VMEM,
        scratch_shapes=[pltpu.VMEM((count + 1, total * NY, LANES), jnp.float32)]
        + [pltpu.VMEM((total * NY, LANES), jnp.float32)] * 5
        + [pltpu.VMEM((2 * count, planes * NY, LANES), jnp.float32)],
        compiler_params=SMALL,
        cost_estimate=pl.CostEstimate(
            flops=apps * NY * LANES * 50,
            bytes_accessed=(count + 1) * total * cells * 4,
            transcendentals=0,
        ),
        name="filter",
    )(jnp.asarray(z_matrix()), *blocks)

    first = flips[:-1]
    early = pl.pallas_call(
        functools.partial(early_kernel, planes=planes, count=count),
        out_shape=jax.ShapeDtypeStruct((2 * count, 2 * chips * planes * count), jnp.float32),
        in_specs=[VMEM] * (1 + 2 * len(first)),
        out_specs=VMEM,
        compiler_params=SMALL,
        name="early",
    )(left, *[near[flip] for flip in first], *[far[flip] for flip in first])

    shares = pl.pallas_call(
        functools.partial(
            late_kernel, planes=planes, count=count, flips=flips, total_cells=total * cells
        ),
        out_shape=jax.ShapeDtypeStruct((doms, 2 * count, LANES), jnp.float32),
        in_specs=[VMEM] * 4,
        out_specs=VMEM,
        compiler_params=SMALL,
        name="late",
    )(left, early, near[flips[-1]], far[flips[-1]])
    parts = [shares[0]] + [along_dom(shares[k], k) for k in range(1, doms)]
    return pl.pallas_call(
        sum_kernel,
        out_shape=jax.ShapeDtypeStruct((2, count, orbs * count // doms), jnp.float32),
        in_specs=[VMEM] * doms,
        out_specs=VMEM,
        compiler_params=SMALL,
        name="total",
    )(*parts)


def with_halo(cells, sides, width):
    for axis, dim in sides:
        count = lax.axis_size(axis)
        head = lax.slice_in_dim(cells, 0, width, axis=dim)
        tail = lax.slice_in_dim(cells, cells.shape[dim] - width, cells.shape[dim], axis=dim)
        cells = jnp.concatenate(
            [
                lax.ppermute(tail, axis, [(i, (i + 1) % count) for i in range(count)]),
                cells,
                lax.ppermute(head, axis, [((i + 1) % count, i) for i in range(count)]),
            ],
            axis=dim,
        )
    return cells


def periodic_pad(cube, axis_index):
    extent = cube.shape[axis_index]
    lower = lax.slice_in_dim(cube, extent - RADIUS, extent, axis=axis_index)
    upper = lax.slice_in_dim(cube, 0, RADIUS, axis=axis_index)
    return jnp.concatenate([lower, cube, upper], axis=axis_index)


def stencil_apply(padded, potential, count):
    offset = (potential.shape[0] - count) // 2
    middle = padded[RADIUS : RADIUS + count]
    width = middle.shape[1]
    cube = middle.reshape(count, width, NY, NZ)
    y_padded = periodic_pad(cube, 2)
    z_padded = periodic_pad(cube, 3)
    lap = 3.0 * coeffs[0] * cube
    for step in range(1, 7):
        near = (
            padded[RADIUS + step : RADIUS + step + count]
            + padded[RADIUS - step : RADIUS - step + count]
        )
        near = near.reshape(count, width, NY, NZ)
        near = (
            near
            + y_padded[:, :, RADIUS - step : RADIUS - step + NY]
            + y_padded[:, :, RADIUS + step : RADIUS + step + NY]
        )
        near = (
            near
            + z_padded[:, :, :, RADIUS - step : RADIUS - step + NZ]
            + z_padded[:, :, :, RADIUS + step : RADIUS + step + NZ]
        )
        lap = lap + coeffs[step] * near
    return (-0.5 * lap).reshape(count, width, NY * NZ) + potential[
        offset : offset + count, None, :
    ] * middle


def apply_field(field, potential):
    padded = with_halo(field, (("dom", 0),), RADIUS)
    return stencil_apply(padded, potential, field.shape[0])


def on_device(orbitals, potential):
    planes = orbitals.shape[0]
    current = (apply_field(orbitals, potential) - center_value * orbitals) / half_value
    following = (
        2.0 * (apply_field(current, potential) - center_value * current) / half_value - orbitals
    )
    applied = apply_field(following, potential)
    filt_cells, appl_cells = (
        lax.all_to_all(following, "orb", split_axis=2, concat_axis=1, tiled=True),
        lax.all_to_all(applied, "orb", split_axis=2, concat_axis=1, tiled=True),
    )
    total_cells = planes * lax.axis_size("dom") * orbitals.shape[2]
    correlation = jnp.einsum(
        "xop,xqp->oq",
        filt_cells,
        filt_cells,
        precision=lax.Precision.HIGHEST,
        preferred_element_type=jnp.float32,
    )
    projected = jnp.einsum(
        "xop,xqp->oq",
        filt_cells,
        appl_cells,
        precision=lax.Precision.HIGHEST,
        preferred_element_type=jnp.float32,
    )
    partial_blocks = jnp.stack([correlation, projected]) / total_cells
    row_blocks = lax.psum_scatter(partial_blocks, "orb", scatter_dimension=1, tiled=True)
    return lax.psum_scatter(row_blocks, "dom", scatter_dimension=2, tiled=True)


def fits_gather(mesh):
    doms, orbs = mesh.shape["dom"], mesh.shape["orb"]
    return orbs == 2 * doms and doms == 4


FLIPS = (1, 2, 3)
CROSS = 1


def solution(mesh):
    gather = fits_gather(mesh)
    return jax.shard_map(
        gathered_device if gather else on_device,
        mesh=mesh,
        in_specs=(P("dom", "orb", None), P("dom", None)),
        out_specs=P(None, "orb", "dom"),
        check_vma=False,
    )
```

```python
import functools

import jax
import jax.numpy as jnp
import numpy as np
from jax import lax
from jax.experimental import pallas as pl
from jax.experimental.pallas import tpu as pltpu
from jax.sharding import PartitionSpec as P


NZ = 96
NY = 8
RADIUS = 6
LANES = 128


coeffs = (
    -5369.0 / 1800.0,
    12.0 / 7.0,
    -15.0 / 56.0,
    10.0 / 189.0,
    -1.0 / 112.0,
    2.0 / 1925.0,
    -1.0 / 16632.0,
)
center_value = 6.5
half_value = 6.5


def turned(tile, shift, axis=1):
    shift = shift % tile.shape[axis]
    return tile if shift == 0 else pltpu.roll(tile, shift, axis)


def line_of(flat, row, lane):
    first, offset = divmod(row * NZ, LANES)
    line = turned(flat[:, first * LANES : (first + 1) * LANES], -offset)
    if offset + NZ > LANES:
        after = turned(flat[:, (first + 1) * LANES : (first + 2) * LANES], -offset)
        line = jnp.where(lane < LANES - offset, line, after)
    return jnp.where(lane < NZ, line, 0.0)


Z_FACTOR = 1.09375


def z_matrix():
    matrix = np.zeros((LANES, LANES), np.float64)
    for cell in range(NZ):
        for step in range(1, RADIUS + 1):
            matrix[cell, (cell + step) % NZ] += coeffs[step] * Z_FACTOR
            matrix[cell, (cell - step) % NZ] += coeffs[step] * Z_FACTOR
    leading = matrix.astype(jnp.bfloat16)
    trailing = (matrix - leading.astype(np.float64)).astype(jnp.bfloat16)
    both = np.concatenate([leading, trailing], axis=1)
    return np.concatenate([both, both], axis=0)


def stencil(load, at, along_z, scale):
    tile = load(at)
    rows = {s: turned(tile, s, 0) + turned(tile, -s, 0) for s in (1, 2, 3)}
    middle = turned(tile, 4, 0)
    rows[4] = middle + middle
    rows[5], rows[6] = rows[3], rows[2]
    total = (scale / Z_FACTOR) * along_z
    for step in range(1, RADIUS + 1):
        near = load(at + step) + load(at - step) + rows[step]
        total = total + (scale * coeffs[step]) * near
    return total


def pack_kernel(orbitals_ref, potential_ref, out_ref, held_ref, sems):
    planes, count, cells = orbitals_ref.shape
    field = pltpu.make_async_copy(orbitals_ref, out_ref.at[pl.ds(0, planes)], sems.at[0])
    level = pltpu.make_async_copy(potential_ref, held_ref, sems.at[1])
    level.start()
    field.start()
    level.wait()
    out_ref[pl.ds(planes, planes // count)] = held_ref[...].reshape(planes // count, count, cells)
    field.wait()


def filter_kernel(matrix_ref, *refs):
    blocks, refs = refs[:-8], refs[-8:]
    out_ref, grid_ref, one_ref, two_ref, three_ref, four_ref, z_ref, save_ref = refs
    count, planes = blocks[0].shape[1], out_ref.shape[0] // (2 * blocks[0].shape[1])
    total = planes * len(blocks)
    lane = lax.broadcasted_iota(jnp.int32, (NY, LANES), 1)

    dom = lax.axis_index("dom")
    for index, block in enumerate(blocks):
        place = pl.multiple_of((((dom ^ index) - dom) & (len(blocks) - 1)) * planes * NY, planes * NY)
        for q in range(count + 1):
            if q < count:
                flat = block[pl.ds(0, planes), q, :]
            else:
                flat = block[pl.ds(planes, planes // count)].reshape(planes, block.shape[2])
            for row in range(NY):
                line = line_of(flat, row, lane)
                if q == count:
                    line = (line - center_value - 1.5 * coeffs[0]) / half_value
                grid_ref[q, pl.ds(place + row, planes, stride=NY), :] = line

    def tile_of(ref):
        def load(at):
            return ref[pl.ds((at % total) * NY, NY), :]

        return load

    def level(at):
        return grid_ref[count, pl.ds((at % total) * NY, NY), :]

    def z_pass(ref, first, number):
        cells = pl.ds(first * NY, number * NY)
        value = ref[cells, :]
        upper = value.astype(jnp.bfloat16)
        lower = (value - upper.astype(jnp.float32)).astype(jnp.bfloat16)
        product = jnp.dot(
            jnp.concatenate([upper, lower], axis=1),
            matrix_ref[...],
            preferred_element_type=jnp.float32,
        )
        z_ref[cells, :] = product[:, :LANES] + product[:, LANES:]

    small = -0.5 / half_value

    def one_orbital(orb, carry):
        start = tile_of(grid_ref.at[orb])
        one, two, three, four = (tile_of(r) for r in (one_ref, two_ref, three_ref, four_ref))
        along_z = tile_of(z_ref)

        def put(ref, at, value):
            ref[pl.ds((at % total) * NY, NY), :] = value

        z_pass(grid_ref.at[orb], 0, total)
        for at in range(total):
            put(one_ref, at, stencil(start, at, along_z(at), small) + level(at) * start(at))
        z_pass(one_ref, 0, total)
        for at in range(total):
            twice = level(at) + level(at)
            value = stencil(one, at, along_z(at), 2.0 * small) + twice * one(at)
            put(two_ref, at, value - start(at))
        z_pass(two_ref, 0, total)
        for at in range(total):
            put(three_ref, at, stencil(two, at, along_z(at), small) + level(at) * two(at))
        z_pass(three_ref, 0, planes + RADIUS)
        z_pass(three_ref, total - RADIUS, RADIUS)
        for at in range(-RADIUS, planes + RADIUS):
            twice = level(at) + level(at)
            value = stencil(three, at, along_z(at), 2.0 * small) + twice * three(at)
            put(four_ref, at, value - two(at))
        z_pass(four_ref, 0, planes)
        for at in range(planes):
            scaled = stencil(four, at, along_z(at), small) + level(at) * four(at)
            save_ref[orb, pl.ds(at * NY, NY), :] = four(at)
            save_ref[count + orb, pl.ds(at * NY, NY), :] = (
                half_value * scaled + center_value * four(at)
            )
        return carry

    lax.fori_loop(0, count, one_orbital, 0)

    rows = 2 * count
    for at in range(planes):
        lines = [save_ref[:, at * NY + row, :] for row in range(NY)]
        for tile in range(NY * NZ // LANES):
            first = tile * LANES
            value = None
            for row in range(NY):
                low, high = max(row * NZ, first), min((row + 1) * NZ, first + LANES)
                if low >= high:
                    continue
                piece = turned(lines[row], row * NZ - first)
                value = piece if value is None else jnp.where(lane < low - first, value, piece)
            out_ref[pl.ds(at * rows, rows), first : first + LANES] = value


def split(value):
    upper = value.astype(jnp.bfloat16)
    lower = (value - upper.astype(jnp.float32)).astype(jnp.bfloat16)
    return upper, lower


def products(left_ref, units, planes):
    rows = left_ref.shape[0] // planes
    left, right = [], []
    for at in range(planes):
        left.append(jnp.concatenate(split(left_ref[pl.ds(at * rows, rows), :]), axis=0))
        lines = jnp.concatenate([unit[at] for unit in units], axis=0)
        right.append(jnp.concatenate(split(lines), axis=0))
    full = lax.dot_general(
        jnp.concatenate(left, axis=1),
        jnp.concatenate(right, axis=1),
        (((1,), (1,)), ((), ())),
        preferred_element_type=jnp.float32,
    )
    full = full[:rows] + full[rows:]
    number = full.shape[1] // 2
    return full[:, :number] + full[:, number:]


def widened(value):
    spare = jnp.zeros((value.shape[0], LANES - value.shape[1]), jnp.float32)
    return jnp.concatenate([value, spare], axis=1)


def near_kernel(left_ref, *refs, planes):
    units, out_ref = refs[:-1], refs[-1]
    out_ref[...] = widened(products(left_ref, units, planes))


def far_kernel(left_ref, near_ref, *refs, planes, flips, total_cells):
    units, out_ref = refs[:-1], refs[-1]
    count = units[0].shape[1]
    near = near_ref[...] * (1.0 / total_cells)
    far = widened(products(left_ref, units, planes)) * (1.0 / total_cells)
    dom, orb = lax.axis_index("dom"), lax.axis_index("orb")
    chip, core = orb >> 1, orb & 1
    even = jnp.where(core == 0, near, far)
    odd = jnp.where(core == 0, far, near)
    lane = lax.broadcasted_iota(jnp.int32, even.shape, 1)
    for slot, flip in enumerate(flips):
        block = jnp.where(
            lane < count, turned(even, -slot * count), turned(odd, (1 - slot) * count)
        )
        out_ref[chip ^ flip ^ dom] = block


def sum_kernel(*refs):
    parts, out_ref = refs[:-1], refs[-1]
    total = parts[0][...]
    for part in parts[1:]:
        total = total + part[...]
    first, rows, columns = out_ref.shape
    for index in range(first):
        out_ref[index] = total[index * rows : (index + 1) * rows, :columns]


VMEM = pl.BlockSpec(memory_space=pltpu.VMEM)
HBM = pl.BlockSpec(memory_space=pltpu.HBM)
SMALL = pltpu.CompilerParams(vmem_limit_bytes=8 << 20)


def gathered_device(orbitals, potential):
    return gathered_steps(orbitals, potential)


def gathered_steps(orbitals, potential):
    doms, orbs = lax.axis_size("dom"), lax.axis_size("orb")
    chips = orbs // 2
    planes, count, cells = orbitals.shape
    total = planes * doms

    def swap_orb(value, flip):
        return lax.ppermute(value, "orb", [(i, i ^ flip) for i in range(orbs)])

    def along_dom(value, step):
        return lax.ppermute(value, "dom", [(i, i ^ step) for i in range(doms)])

    packed = pl.pallas_call(
        pack_kernel,
        out_shape=jax.ShapeDtypeStruct((planes + planes // count, count, cells), jnp.float32),
        in_specs=[HBM, HBM],
        out_specs=VMEM,
        scratch_shapes=[pltpu.VMEM((planes, cells), jnp.float32), pltpu.SemaphoreType.DMA((2,))],
        compiler_params=SMALL,
        name="pack",
    )(
        pltpu.with_memory_space_constraint(orbitals, pltpu.HBM),
        pltpu.with_memory_space_constraint(potential, pltpu.HBM),
    )
    others = {step: along_dom(packed, step) for step in range(1, doms)}
    blocks = [packed] + [others[step] for step in range(1, doms)]

    flips = (0, *FLIPS) if chips == 1 + len(FLIPS) else tuple(range(chips))
    near = {0: packed}
    for flip in flips[1:]:
        near[flip] = swap_orb(orbitals, 2 * flip)
    far = {0: swap_orb(orbitals, 1)}
    for flip in flips[1:]:
        if flip == CROSS:
            far[flip] = swap_orb(orbitals, 2 * flip + 1)
        else:
            far[flip] = swap_orb(near[flip], 1)

    apps = count * (3 * total + 2 * planes + 2 * RADIUS)
    left = pl.pallas_call(
        filter_kernel,
        out_shape=jax.ShapeDtypeStruct((planes * 2 * count, cells), jnp.float32),
        in_specs=[VMEM] * (1 + doms),
        out_specs=VMEM,
        scratch_shapes=[pltpu.VMEM((count + 1, total * NY, LANES), jnp.float32)]
        + [pltpu.VMEM((total * NY, LANES), jnp.float32)] * 5
        + [pltpu.VMEM((2 * count, planes * NY, LANES), jnp.float32)],
        compiler_params=SMALL,
        cost_estimate=pl.CostEstimate(
            flops=apps * NY * LANES * 50,
            bytes_accessed=(count + 1) * total * cells * 4,
            transcendentals=0,
        ),
        name="filter",
    )(jnp.asarray(z_matrix()), *blocks)

    early = pl.pallas_call(
        functools.partial(near_kernel, planes=planes),
        out_shape=jax.ShapeDtypeStruct((2 * count, LANES), jnp.float32),
        in_specs=[VMEM] * (1 + chips),
        out_specs=VMEM,
        compiler_params=SMALL,
        name="early",
    )(left, *[near[flip] for flip in flips])

    shares = pl.pallas_call(
        functools.partial(far_kernel, planes=planes, flips=flips, total_cells=total * cells),
        out_shape=jax.ShapeDtypeStruct((doms, 2 * count, LANES), jnp.float32),
        in_specs=[VMEM] * (2 + chips),
        out_specs=VMEM,
        compiler_params=SMALL,
        name="late",
    )(left, early, *[far[flip] for flip in flips])
    parts = [shares[0]] + [along_dom(shares[k], k) for k in range(1, doms)]
    return pl.pallas_call(
        sum_kernel,
        out_shape=jax.ShapeDtypeStruct((2, count, orbs * count // doms), jnp.float32),
        in_specs=[VMEM] * doms,
        out_specs=VMEM,
        compiler_params=SMALL,
        name="total",
    )(*parts)


def with_halo(cells, sides, width):
    for axis, dim in sides:
        count = lax.axis_size(axis)
        head = lax.slice_in_dim(cells, 0, width, axis=dim)
        tail = lax.slice_in_dim(cells, cells.shape[dim] - width, cells.shape[dim], axis=dim)
        cells = jnp.concatenate(
            [
                lax.ppermute(tail, axis, [(i, (i + 1) % count) for i in range(count)]),
                cells,
                lax.ppermute(head, axis, [((i + 1) % count, i) for i in range(count)]),
            ],
            axis=dim,
        )
    return cells


def periodic_pad(cube, axis_index):
    extent = cube.shape[axis_index]
    lower = lax.slice_in_dim(cube, extent - RADIUS, extent, axis=axis_index)
    upper = lax.slice_in_dim(cube, 0, RADIUS, axis=axis_index)
    return jnp.concatenate([lower, cube, upper], axis=axis_index)


def stencil_apply(padded, potential, count):
    offset = (potential.shape[0] - count) // 2
    middle = padded[RADIUS : RADIUS + count]
    width = middle.shape[1]
    cube = middle.reshape(count, width, NY, NZ)
    y_padded = periodic_pad(cube, 2)
    z_padded = periodic_pad(cube, 3)
    lap = 3.0 * coeffs[0] * cube
    for step in range(1, 7):
        near = (
            padded[RADIUS + step : RADIUS + step + count]
            + padded[RADIUS - step : RADIUS - step + count]
        )
        near = near.reshape(count, width, NY, NZ)
        near = (
            near
            + y_padded[:, :, RADIUS - step : RADIUS - step + NY]
            + y_padded[:, :, RADIUS + step : RADIUS + step + NY]
        )
        near = (
            near
            + z_padded[:, :, :, RADIUS - step : RADIUS - step + NZ]
            + z_padded[:, :, :, RADIUS + step : RADIUS + step + NZ]
        )
        lap = lap + coeffs[step] * near
    return (-0.5 * lap).reshape(count, width, NY * NZ) + potential[
        offset : offset + count, None, :
    ] * middle


def apply_field(field, potential):
    padded = with_halo(field, (("dom", 0),), RADIUS)
    return stencil_apply(padded, potential, field.shape[0])


def on_device(orbitals, potential):
    planes = orbitals.shape[0]
    current = (apply_field(orbitals, potential) - center_value * orbitals) / half_value
    following = (
        2.0 * (apply_field(current, potential) - center_value * current) / half_value - orbitals
    )
    applied = apply_field(following, potential)
    filt_cells, appl_cells = (
        lax.all_to_all(following, "orb", split_axis=2, concat_axis=1, tiled=True),
        lax.all_to_all(applied, "orb", split_axis=2, concat_axis=1, tiled=True),
    )
    total_cells = planes * lax.axis_size("dom") * orbitals.shape[2]
    correlation = jnp.einsum(
        "xop,xqp->oq",
        filt_cells,
        filt_cells,
        precision=lax.Precision.HIGHEST,
        preferred_element_type=jnp.float32,
    )
    projected = jnp.einsum(
        "xop,xqp->oq",
        filt_cells,
        appl_cells,
        precision=lax.Precision.HIGHEST,
        preferred_element_type=jnp.float32,
    )
    partial_blocks = jnp.stack([correlation, projected]) / total_cells
    row_blocks = lax.psum_scatter(partial_blocks, "orb", scatter_dimension=1, tiled=True)
    return lax.psum_scatter(row_blocks, "dom", scatter_dimension=2, tiled=True)


def fits_gather(mesh):
    doms, orbs = mesh.shape["dom"], mesh.shape["orb"]
    return orbs == 2 * doms and doms == 4


FLIPS = (1, 2, 3)
CROSS = 1


def solution(mesh):
    gather = fits_gather(mesh)
    return jax.shard_map(
        gathered_device if gather else on_device,
        mesh=mesh,
        in_specs=(P("dom", "orb", None), P("dom", None)),
        out_specs=P(None, "orb", "dom"),
        check_vma=False,
    )
```

```python
import functools

import jax
import jax.numpy as jnp
import numpy as np
from jax import lax
from jax.experimental import pallas as pl
from jax.experimental.pallas import tpu as pltpu
from jax.sharding import PartitionSpec as P


NZ = 96
NY = 8
RADIUS = 6
LANES = 128


coeffs = (
    -5369.0 / 1800.0,
    12.0 / 7.0,
    -15.0 / 56.0,
    10.0 / 189.0,
    -1.0 / 112.0,
    2.0 / 1925.0,
    -1.0 / 16632.0,
)
center_value = 6.5
half_value = 6.5


GROUP = 4


def turned(tile, shift, axis=1):
    shift = shift % tile.shape[axis]
    return tile if shift == 0 else pltpu.roll(tile, shift, axis)


def line_of(flat, row, lane):
    first, offset = divmod(row * NZ, LANES)
    line = turned(flat[:, first * LANES : (first + 1) * LANES], -offset)
    if offset + NZ > LANES:
        after = turned(flat[:, (first + 1) * LANES : (first + 2) * LANES], -offset)
        line = jnp.where(lane < LANES - offset, line, after)
    return jnp.where(lane < NZ, line, 0.0)


Z_FACTOR = 1.09375


def z_matrix():
    matrix = np.zeros((LANES, LANES), np.float64)
    for cell in range(NZ):
        for step in range(1, RADIUS + 1):
            matrix[cell, (cell + step) % NZ] += coeffs[step] * Z_FACTOR
            matrix[cell, (cell - step) % NZ] += coeffs[step] * Z_FACTOR
    leading = matrix.astype(jnp.bfloat16)
    trailing = (matrix - leading.astype(np.float64)).astype(jnp.bfloat16)
    both = np.concatenate([leading, trailing], axis=1)
    return np.concatenate([both, both], axis=0)


def stencil(load, at, along_z, scale):
    tile = load(at)
    rows = {s: turned(tile, s, 0) + turned(tile, -s, 0) for s in (1, 2, 3)}
    middle = turned(tile, 4, 0)
    rows[4] = middle + middle
    rows[5], rows[6] = rows[3], rows[2]
    total = (scale / Z_FACTOR) * along_z
    for step in range(1, RADIUS + 1):
        near = load(at + step) + load(at - step) + rows[step]
        total = total + (scale * coeffs[step]) * near
    return total


def pack_kernel(orbitals_ref, potential_ref, out_ref, held_ref, sems):
    planes, count, cells = orbitals_ref.shape
    field = pltpu.make_async_copy(orbitals_ref, out_ref.at[pl.ds(0, planes)], sems.at[0])
    level = pltpu.make_async_copy(potential_ref, held_ref, sems.at[1])
    level.start()
    field.start()
    level.wait()
    out_ref[pl.ds(planes, planes // count)] = held_ref[...].reshape(planes // count, count, cells)
    field.wait()


def filter_kernel(matrix_ref, *refs):
    blocks, refs = refs[:-8], refs[-8:]
    out_ref, grid_ref, one_ref, two_ref, three_ref, four_ref, z_ref, save_ref = refs
    count, planes = blocks[0].shape[1], out_ref.shape[0] // (2 * blocks[0].shape[1])
    total = planes * len(blocks)
    lane = lax.broadcasted_iota(jnp.int32, (NY, LANES), 1)

    dom = lax.axis_index("dom")
    for index, block in enumerate(blocks):
        place = pl.multiple_of((((dom ^ index) - dom) & (len(blocks) - 1)) * planes * NY, planes * NY)
        for q in range(count + 1):
            if q < count:
                flat = block[pl.ds(0, planes), q, :]
            else:
                flat = block[pl.ds(planes, planes // count)].reshape(planes, block.shape[2])
            for row in range(NY):
                line = line_of(flat, row, lane)
                if q == count:
                    line = (line - center_value - 1.5 * coeffs[0]) / half_value
                grid_ref[q, pl.ds(place + row, planes, stride=NY), :] = line

    def tile_of(ref):
        def load(at):
            return ref[pl.ds((at % total) * NY, NY), :]

        return load

    def level(at):
        return grid_ref[count, pl.ds((at % total) * NY, NY), :]

    def z_pass(ref, out, first, number):
        cells = pl.ds(first * NY, number * NY)
        value = ref[cells, :]
        upper = value.astype(jnp.bfloat16)
        lower = (value - upper.astype(jnp.float32)).astype(jnp.bfloat16)
        product = jnp.dot(
            jnp.concatenate([upper, lower], axis=1),
            matrix_ref[...],
            preferred_element_type=jnp.float32,
        )
        out[cells, :] = product[:, :LANES] + product[:, LANES:]

    small = -0.5 / half_value

    group = one_ref.shape[0]

    def orbitals_of(turn, carry):
        orbs = [turn * group + slot for slot in range(group)]
        fields = [grid_ref.at[orb] for orb in orbs]
        levels_of = [fields] + [
            [ref.at[slot] for slot in range(group)] for ref in (one_ref, two_ref, three_ref, four_ref)
        ]
        z_refs = [z_ref.at[slot] for slot in range(group)]
        start, one, two, three, four = ([tile_of(r) for r in refs] for refs in levels_of)

        def put(ref, at, value):
            ref[pl.ds((at % total) * NY, NY), :] = value

        def along(slot, at):
            return z_refs[slot][pl.ds((at % total) * NY, NY), :]

        def passes(refs, *spans):
            for slot in range(group):
                for first, number in spans:
                    z_pass(refs[slot], z_refs[slot], first, number)

        passes(levels_of[0], (0, total))
        for slot in range(group):
            f = start[slot]
            for at in range(total):
                value = stencil(f, at, along(slot, at), small) + level(at) * f(at)
                put(levels_of[1][slot], at, value)
        passes(levels_of[1], (0, total))
        for slot in range(group):
            f = one[slot]
            for at in range(total):
                twice = level(at) + level(at)
                value = stencil(f, at, along(slot, at), 2.0 * small) + twice * f(at)
                put(levels_of[2][slot], at, value - start[slot](at))
        passes(levels_of[2], (0, total))
        for slot in range(group):
            f = two[slot]
            for at in range(total):
                value = stencil(f, at, along(slot, at), small) + level(at) * f(at)
                put(levels_of[3][slot], at, value)
        passes(levels_of[3], (0, planes + RADIUS), (total - RADIUS, RADIUS))
        for slot in range(group):
            f = three[slot]
            for at in range(-RADIUS, planes + RADIUS):
                twice = level(at) + level(at)
                value = stencil(f, at, along(slot, at), 2.0 * small) + twice * f(at)
                put(levels_of[4][slot], at, value - two[slot](at))
        passes(levels_of[4], (0, planes))
        for slot in range(group):
            f = four[slot]
            for at in range(planes):
                scaled = stencil(f, at, along(slot, at), small) + level(at) * f(at)
                held = pl.multiple_of(orbs[slot] * (planes * NY), planes * NY) + at * NY
                save_ref[pl.ds(held, NY), :] = f(at)
                save_ref[pl.ds(held + count * planes * NY, NY), :] = (
                    half_value * scaled + center_value * f(at)
                )
        return carry

    lax.fori_loop(0, count // group, orbitals_of, 0)

    rows = 2 * count
    for at in range(planes):
        lines = [
            save_ref[pl.ds(at * NY + row, rows, stride=planes * NY), :] for row in range(NY)
        ]
        for tile in range(NY * NZ // LANES):
            first = tile * LANES
            value = None
            for row in range(NY):
                low, high = max(row * NZ, first), min((row + 1) * NZ, first + LANES)
                if low >= high:
                    continue
                piece = turned(lines[row], row * NZ - first)
                value = piece if value is None else jnp.where(lane < low - first, value, piece)
            out_ref[pl.ds(at * rows, rows), first : first + LANES] = value


def split(value):
    upper = value.astype(jnp.bfloat16)
    lower = (value - upper.astype(jnp.float32)).astype(jnp.bfloat16)
    return upper, lower


def products(left_ref, units, planes):
    rows = left_ref.shape[0] // planes
    left, right = [], []
    for at in range(planes):
        left.append(jnp.concatenate(split(left_ref[pl.ds(at * rows, rows), :]), axis=0))
        lines = jnp.concatenate([unit[at] for unit in units], axis=0)
        right.append(jnp.concatenate(split(lines), axis=0))
    full = lax.dot_general(
        jnp.concatenate(left, axis=1),
        jnp.concatenate(right, axis=1),
        (((1,), (1,)), ((), ())),
        preferred_element_type=jnp.float32,
    )
    full = full[:rows] + full[rows:]
    number = full.shape[1] // 2
    return full[:, :number] + full[:, number:]


def widened(value):
    spare = jnp.zeros((value.shape[0], LANES - value.shape[1]), jnp.float32)
    return jnp.concatenate([value, spare], axis=1)


def near_kernel(left_ref, *refs, planes):
    units, out_ref = refs[:-1], refs[-1]
    out_ref[...] = widened(products(left_ref, units, planes))


def far_kernel(left_ref, near_ref, *refs, planes, flips, total_cells):
    units, out_ref = refs[:-1], refs[-1]
    count = units[0].shape[1]
    near = near_ref[...] * (1.0 / total_cells)
    far = widened(products(left_ref, units, planes)) * (1.0 / total_cells)
    dom, orb = lax.axis_index("dom"), lax.axis_index("orb")
    chip, core = orb >> 1, orb & 1
    even = jnp.where(core == 0, near, far)
    odd = jnp.where(core == 0, far, near)
    lane = lax.broadcasted_iota(jnp.int32, even.shape, 1)
    for slot, flip in enumerate(flips):
        block = jnp.where(
            lane < count, turned(even, -slot * count), turned(odd, (1 - slot) * count)
        )
        out_ref[chip ^ flip ^ dom] = block


def sum_kernel(*refs):
    parts, out_ref = refs[:-1], refs[-1]
    total = parts[0][...]
    for part in parts[1:]:
        total = total + part[...]
    first, rows, columns = out_ref.shape
    for index in range(first):
        out_ref[index] = total[index * rows : (index + 1) * rows, :columns]


VMEM = pl.BlockSpec(memory_space=pltpu.VMEM)
HBM = pl.BlockSpec(memory_space=pltpu.HBM)
SMALL = pltpu.CompilerParams(vmem_limit_bytes=8 << 20)


def gathered_device(orbitals, potential):
    return gathered_steps(orbitals, potential)


def gathered_steps(orbitals, potential):
    doms, orbs = lax.axis_size("dom"), lax.axis_size("orb")
    chips = orbs // 2
    planes, count, cells = orbitals.shape
    total = planes * doms

    def swap_orb(value, flip):
        return lax.ppermute(value, "orb", [(i, i ^ flip) for i in range(orbs)])

    def along_dom(value, step):
        return lax.ppermute(value, "dom", [(i, i ^ step) for i in range(doms)])

    packed = pl.pallas_call(
        pack_kernel,
        out_shape=jax.ShapeDtypeStruct((planes + planes // count, count, cells), jnp.float32),
        in_specs=[HBM, HBM],
        out_specs=VMEM,
        scratch_shapes=[pltpu.VMEM((planes, cells), jnp.float32), pltpu.SemaphoreType.DMA((2,))],
        compiler_params=SMALL,
        name="pack",
    )(
        pltpu.with_memory_space_constraint(orbitals, pltpu.HBM),
        pltpu.with_memory_space_constraint(potential, pltpu.HBM),
    )
    others = {step: along_dom(packed, step) for step in range(1, doms)}
    blocks = [packed] + [others[step] for step in range(1, doms)]

    flips = tuple(range(chips))
    near = {0: packed, 2: swap_orb(orbitals, 4), 1: swap_orb(orbitals, 2)}
    near[3] = swap_orb(near[2], 2)
    far = {
        0: swap_orb(orbitals, 1),
        1: swap_orb(orbitals, 3) if CROSS == 1 else swap_orb(near[1], 1),
        2: swap_orb(near[2], 1),
        3: swap_orb(near[2], 3) if RELAYED else swap_orb(near[3], 1),
    }

    apps = count * (3 * total + 2 * planes + 2 * RADIUS)
    left = pl.pallas_call(
        filter_kernel,
        out_shape=jax.ShapeDtypeStruct((planes * 2 * count, cells), jnp.float32),
        in_specs=[VMEM] * (1 + doms),
        out_specs=VMEM,
        scratch_shapes=[pltpu.VMEM((count + 1, total * NY, LANES), jnp.float32)]
        + [pltpu.VMEM((GROUP, total * NY, LANES), jnp.float32)] * 5
        + [pltpu.VMEM((2 * count * planes * NY, LANES), jnp.float32)],
        compiler_params=SMALL,
        cost_estimate=pl.CostEstimate(
            flops=apps * NY * LANES * 50,
            bytes_accessed=(count + 1) * total * cells * 4,
            transcendentals=0,
        ),
        name="filter",
    )(jnp.asarray(z_matrix()), *blocks)

    early = pl.pallas_call(
        functools.partial(near_kernel, planes=planes),
        out_shape=jax.ShapeDtypeStruct((2 * count, LANES), jnp.float32),
        in_specs=[VMEM] * (1 + chips),
        out_specs=VMEM,
        compiler_params=SMALL,
        name="early",
    )(left, *[near[flip] for flip in flips])

    shares = pl.pallas_call(
        functools.partial(far_kernel, planes=planes, flips=flips, total_cells=total * cells),
        out_shape=jax.ShapeDtypeStruct((doms, 2 * count, LANES), jnp.float32),
        in_specs=[VMEM] * (2 + chips),
        out_specs=VMEM,
        compiler_params=SMALL,
        name="late",
    )(left, early, *[far[flip] for flip in flips])
    parts = [shares[0]] + [along_dom(shares[k], k) for k in range(1, doms)]
    return pl.pallas_call(
        sum_kernel,
        out_shape=jax.ShapeDtypeStruct((2, count, orbs * count // doms), jnp.float32),
        in_specs=[VMEM] * doms,
        out_specs=VMEM,
        compiler_params=SMALL,
        name="total",
    )(*parts)


def with_halo(cells, sides, width):
    for axis, dim in sides:
        count = lax.axis_size(axis)
        head = lax.slice_in_dim(cells, 0, width, axis=dim)
        tail = lax.slice_in_dim(cells, cells.shape[dim] - width, cells.shape[dim], axis=dim)
        cells = jnp.concatenate(
            [
                lax.ppermute(tail, axis, [(i, (i + 1) % count) for i in range(count)]),
                cells,
                lax.ppermute(head, axis, [((i + 1) % count, i) for i in range(count)]),
            ],
            axis=dim,
        )
    return cells


def periodic_pad(cube, axis_index):
    extent = cube.shape[axis_index]
    lower = lax.slice_in_dim(cube, extent - RADIUS, extent, axis=axis_index)
    upper = lax.slice_in_dim(cube, 0, RADIUS, axis=axis_index)
    return jnp.concatenate([lower, cube, upper], axis=axis_index)


def stencil_apply(padded, potential, count):
    offset = (potential.shape[0] - count) // 2
    middle = padded[RADIUS : RADIUS + count]
    width = middle.shape[1]
    cube = middle.reshape(count, width, NY, NZ)
    y_padded = periodic_pad(cube, 2)
    z_padded = periodic_pad(cube, 3)
    lap = 3.0 * coeffs[0] * cube
    for step in range(1, 7):
        near = (
            padded[RADIUS + step : RADIUS + step + count]
            + padded[RADIUS - step : RADIUS - step + count]
        )
        near = near.reshape(count, width, NY, NZ)
        near = (
            near
            + y_padded[:, :, RADIUS - step : RADIUS - step + NY]
            + y_padded[:, :, RADIUS + step : RADIUS + step + NY]
        )
        near = (
            near
            + z_padded[:, :, :, RADIUS - step : RADIUS - step + NZ]
            + z_padded[:, :, :, RADIUS + step : RADIUS + step + NZ]
        )
        lap = lap + coeffs[step] * near
    return (-0.5 * lap).reshape(count, width, NY * NZ) + potential[
        offset : offset + count, None, :
    ] * middle


def apply_field(field, potential):
    padded = with_halo(field, (("dom", 0),), RADIUS)
    return stencil_apply(padded, potential, field.shape[0])


def on_device(orbitals, potential):
    planes = orbitals.shape[0]
    current = (apply_field(orbitals, potential) - center_value * orbitals) / half_value
    following = (
        2.0 * (apply_field(current, potential) - center_value * current) / half_value - orbitals
    )
    applied = apply_field(following, potential)
    filt_cells, appl_cells = (
        lax.all_to_all(following, "orb", split_axis=2, concat_axis=1, tiled=True),
        lax.all_to_all(applied, "orb", split_axis=2, concat_axis=1, tiled=True),
    )
    total_cells = planes * lax.axis_size("dom") * orbitals.shape[2]
    correlation = jnp.einsum(
        "xop,xqp->oq",
        filt_cells,
        filt_cells,
        precision=lax.Precision.HIGHEST,
        preferred_element_type=jnp.float32,
    )
    projected = jnp.einsum(
        "xop,xqp->oq",
        filt_cells,
        appl_cells,
        precision=lax.Precision.HIGHEST,
        preferred_element_type=jnp.float32,
    )
    partial_blocks = jnp.stack([correlation, projected]) / total_cells
    row_blocks = lax.psum_scatter(partial_blocks, "orb", scatter_dimension=1, tiled=True)
    return lax.psum_scatter(row_blocks, "dom", scatter_dimension=2, tiled=True)


def fits_gather(mesh):
    doms, orbs = mesh.shape["dom"], mesh.shape["orb"]
    return orbs == 2 * doms and doms == 4


CROSS = 0
RELAYED = True


def solution(mesh):
    gather = fits_gather(mesh)
    return jax.shard_map(
        gathered_device if gather else on_device,
        mesh=mesh,
        in_specs=(P("dom", "orb", None), P("dom", None)),
        out_specs=P(None, "orb", "dom"),
        check_vma=False,
    )
```

```python
import functools

import jax
import jax.numpy as jnp
import numpy as np
from jax import lax
from jax.experimental import pallas as pl
from jax.experimental.pallas import tpu as pltpu
from jax.sharding import PartitionSpec as P


NZ = 96
NY = 8
RADIUS = 6
LANES = 128


coeffs = (
    -5369.0 / 1800.0,
    12.0 / 7.0,
    -15.0 / 56.0,
    10.0 / 189.0,
    -1.0 / 112.0,
    2.0 / 1925.0,
    -1.0 / 16632.0,
)
center_value = 6.5
half_value = 6.5


GROUP = 4


def turned(tile, shift, axis=1):
    shift = shift % tile.shape[axis]
    return tile if shift == 0 else pltpu.roll(tile, shift, axis)


def line_of(flat, row, lane):
    first, offset = divmod(row * NZ, LANES)
    line = turned(flat[:, first * LANES : (first + 1) * LANES], -offset)
    if offset + NZ > LANES:
        after = turned(flat[:, (first + 1) * LANES : (first + 2) * LANES], -offset)
        line = jnp.where(lane < LANES - offset, line, after)
    return jnp.where(lane < NZ, line, 0.0)


Z_FACTOR = -0.5 / half_value


def z_matrix():
    matrix = np.zeros((LANES, LANES), np.float64)
    for cell in range(NZ):
        for step in range(1, RADIUS + 1):
            matrix[cell, (cell + step) % NZ] += coeffs[step] * Z_FACTOR
            matrix[cell, (cell - step) % NZ] += coeffs[step] * Z_FACTOR
    leading = matrix.astype(jnp.bfloat16)
    trailing = (matrix - leading.astype(np.float64)).astype(jnp.bfloat16)
    both = np.concatenate([leading, trailing], axis=1)
    return np.concatenate([both, both], axis=0)


def stencil(load, at, along_z, scale):
    tile = load(at)
    rows = {s: turned(tile, s, 0) + turned(tile, -s, 0) for s in (1, 2, 3)}
    middle = turned(tile, 4, 0)
    rows[4] = middle + middle
    rows[5], rows[6] = rows[3], rows[2]
    total = along_z
    for step in range(1, RADIUS + 1):
        near = load(at + step) + load(at - step) + rows[step]
        total = total + (scale * coeffs[step]) * near
    return total


def pack_kernel(orbitals_ref, potential_ref, out_ref, held_ref, sems):
    planes, count, cells = orbitals_ref.shape
    field = pltpu.make_async_copy(orbitals_ref, out_ref.at[pl.ds(0, planes)], sems.at[0])
    level = pltpu.make_async_copy(potential_ref, held_ref, sems.at[1])
    level.start()
    field.start()
    level.wait()
    out_ref[pl.ds(planes, planes // count)] = held_ref[...].reshape(planes // count, count, cells)
    field.wait()


def filter_kernel(matrix_ref, *refs):
    blocks, refs = refs[:-8], refs[-8:]
    out_ref, grid_ref, one_ref, two_ref, three_ref, four_ref, z_ref, save_ref = refs
    count, planes = blocks[0].shape[1], out_ref.shape[0] // (2 * blocks[0].shape[1])
    total = planes * len(blocks)
    lane = lax.broadcasted_iota(jnp.int32, (NY, LANES), 1)

    dom = lax.axis_index("dom")
    for index, block in enumerate(blocks):
        place = pl.multiple_of((((dom ^ index) - dom) & (len(blocks) - 1)) * planes * NY, planes * NY)
        for q in range(count + 1):
            if q < count:
                flat = block[pl.ds(0, planes), q, :]
            else:
                flat = block[pl.ds(planes, planes // count)].reshape(planes, block.shape[2])
            for row in range(NY):
                line = line_of(flat, row, lane)
                if q == count:
                    line = (line - center_value - 1.5 * coeffs[0]) / half_value
                grid_ref[q, pl.ds(place + row, planes, stride=NY), :] = line

    def tile_of(ref):
        def load(at):
            return ref[pl.ds((at % total) * NY, NY), :]

        return load

    def level(at):
        return grid_ref[count, pl.ds((at % total) * NY, NY), :]

    def z_pass(ref, out, first, number):
        cells = pl.ds(first * NY, number * NY)
        value = ref[cells, :]
        upper = value.astype(jnp.bfloat16)
        lower = (value - upper.astype(jnp.float32)).astype(jnp.bfloat16)
        product = jnp.dot(
            jnp.concatenate([upper, lower], axis=1),
            matrix_ref[...],
            preferred_element_type=jnp.float32,
        )
        out[cells, :] = product[:, :LANES] + product[:, LANES:]

    small = -0.5 / half_value

    group = one_ref.shape[0]

    def orbitals_of(turn, carry):
        orbs = [turn * group + slot for slot in range(group)]
        fields = [grid_ref.at[orb] for orb in orbs]
        levels_of = [fields] + [
            [ref.at[slot] for slot in range(group)] for ref in (one_ref, two_ref, three_ref, four_ref)
        ]
        z_refs = [z_ref.at[slot] for slot in range(group)]
        start, one, two, three, four = ([tile_of(r) for r in refs] for refs in levels_of)

        def put(ref, at, value):
            ref[pl.ds((at % total) * NY, NY), :] = value

        def along(slot, at):
            return z_refs[slot][pl.ds((at % total) * NY, NY), :]

        def passes(refs, *spans):
            for slot in range(group):
                for first, number in spans:
                    z_pass(refs[slot], z_refs[slot], first, number)

        passes(levels_of[0], (0, total))
        for slot in range(group):
            f = start[slot]
            for at in range(total):
                value = stencil(f, at, along(slot, at), small) + level(at) * f(at)
                put(levels_of[1][slot], at, value)
        passes(levels_of[1], (0, total))
        for slot in range(group):
            f = one[slot]
            for at in range(total):
                value = stencil(f, at, along(slot, at), small) + level(at) * f(at)
                put(levels_of[2][slot], at, (value + value) - start[slot](at))
        passes(levels_of[2], (0, total))
        for slot in range(group):
            f = two[slot]
            for at in range(total):
                value = stencil(f, at, along(slot, at), small) + level(at) * f(at)
                put(levels_of[3][slot], at, value)
        passes(levels_of[3], (0, planes + RADIUS), (total - RADIUS, RADIUS))
        for slot in range(group):
            f = three[slot]
            for at in range(-RADIUS, planes + RADIUS):
                value = stencil(f, at, along(slot, at), small) + level(at) * f(at)
                put(levels_of[4][slot], at, (value + value) - two[slot](at))
        passes(levels_of[4], (0, planes))
        for slot in range(group):
            f = four[slot]
            for at in range(planes):
                scaled = stencil(f, at, along(slot, at), small) + level(at) * f(at)
                held = pl.multiple_of(orbs[slot] * (planes * NY), planes * NY) + at * NY
                save_ref[pl.ds(held, NY), :] = f(at)
                save_ref[pl.ds(held + count * planes * NY, NY), :] = (
                    half_value * scaled + center_value * f(at)
                )
        return carry

    lax.fori_loop(0, count // group, orbitals_of, 0)

    rows = 2 * count
    for at in range(planes):
        lines = [
            save_ref[pl.ds(at * NY + row, rows, stride=planes * NY), :] for row in range(NY)
        ]
        for tile in range(NY * NZ // LANES):
            first = tile * LANES
            value = None
            for row in range(NY):
                low, high = max(row * NZ, first), min((row + 1) * NZ, first + LANES)
                if low >= high:
                    continue
                piece = turned(lines[row], row * NZ - first)
                value = piece if value is None else jnp.where(lane < low - first, value, piece)
            out_ref[pl.ds(at * rows, rows), first : first + LANES] = value


def split(value):
    upper = value.astype(jnp.bfloat16)
    lower = (value - upper.astype(jnp.float32)).astype(jnp.bfloat16)
    return upper, lower


def products(left_ref, units, planes):
    rows = left_ref.shape[0] // planes
    left, right = [], []
    for at in range(planes):
        left.append(jnp.concatenate(split(left_ref[pl.ds(at * rows, rows), :]), axis=0))
        lines = jnp.concatenate([unit[at] for unit in units], axis=0)
        right.append(jnp.concatenate(split(lines), axis=0))
    full = lax.dot_general(
        jnp.concatenate(left, axis=1),
        jnp.concatenate(right, axis=1),
        (((1,), (1,)), ((), ())),
        preferred_element_type=jnp.float32,
    )
    full = full[:rows] + full[rows:]
    number = full.shape[1] // 2
    return full[:, :number] + full[:, number:]


def widened(value):
    spare = jnp.zeros((value.shape[0], LANES - value.shape[1]), jnp.float32)
    return jnp.concatenate([value, spare], axis=1)


def near_kernel(left_ref, *refs, planes):
    units, out_ref = refs[:-1], refs[-1]
    out_ref[...] = widened(products(left_ref, units, planes))


def far_kernel(left_ref, near_ref, *refs, planes, flips, total_cells):
    units, out_ref = refs[:-1], refs[-1]
    count = units[0].shape[1]
    near = near_ref[...] * (1.0 / total_cells)
    far = widened(products(left_ref, units, planes)) * (1.0 / total_cells)
    dom, orb = lax.axis_index("dom"), lax.axis_index("orb")
    chip, core = orb >> 1, orb & 1
    even = jnp.where(core == 0, near, far)
    odd = jnp.where(core == 0, far, near)
    lane = lax.broadcasted_iota(jnp.int32, even.shape, 1)
    for slot, flip in enumerate(flips):
        block = jnp.where(
            lane < count, turned(even, -slot * count), turned(odd, (1 - slot) * count)
        )
        out_ref[chip ^ flip ^ dom] = block


def sum_kernel(*refs):
    parts, out_ref = refs[:-1], refs[-1]
    total = parts[0][...]
    for part in parts[1:]:
        total = total + part[...]
    first, rows, columns = out_ref.shape
    for index in range(first):
        out_ref[index] = total[index * rows : (index + 1) * rows, :columns]


VMEM = pl.BlockSpec(memory_space=pltpu.VMEM)
HBM = pl.BlockSpec(memory_space=pltpu.HBM)
SMALL = pltpu.CompilerParams(vmem_limit_bytes=8 << 20)


def gathered_device(orbitals, potential):
    return gathered_steps(orbitals, potential)


def gathered_steps(orbitals, potential):
    doms, orbs = lax.axis_size("dom"), lax.axis_size("orb")
    chips = orbs // 2
    planes, count, cells = orbitals.shape
    total = planes * doms

    def swap_orb(value, flip):
        return lax.ppermute(value, "orb", [(i, i ^ flip) for i in range(orbs)])

    def along_dom(value, step):
        return lax.ppermute(value, "dom", [(i, i ^ step) for i in range(doms)])

    packed = pl.pallas_call(
        pack_kernel,
        out_shape=jax.ShapeDtypeStruct((planes + planes // count, count, cells), jnp.float32),
        in_specs=[HBM, HBM],
        out_specs=VMEM,
        scratch_shapes=[pltpu.VMEM((planes, cells), jnp.float32), pltpu.SemaphoreType.DMA((2,))],
        compiler_params=SMALL,
        name="pack",
    )(
        pltpu.with_memory_space_constraint(orbitals, pltpu.HBM),
        pltpu.with_memory_space_constraint(potential, pltpu.HBM),
    )
    others = {step: along_dom(packed, step) for step in range(1, doms)}
    blocks = [packed] + [others[step] for step in range(1, doms)]

    flips = tuple(range(chips))
    near = {0: packed, 2: swap_orb(orbitals, 4), 1: swap_orb(orbitals, 2)}
    near[3] = swap_orb(near[2], 2)
    far = {
        0: swap_orb(orbitals, 1),
        1: swap_orb(orbitals, 3) if CROSS == 1 else swap_orb(near[1], 1),
        2: swap_orb(near[2], 1),
        3: swap_orb(near[2], 3) if RELAYED else swap_orb(near[3], 1),
    }

    apps = count * (3 * total + 2 * planes + 2 * RADIUS)
    left = pl.pallas_call(
        filter_kernel,
        out_shape=jax.ShapeDtypeStruct((planes * 2 * count, cells), jnp.float32),
        in_specs=[VMEM] * (1 + doms),
        out_specs=VMEM,
        scratch_shapes=[pltpu.VMEM((count + 1, total * NY, LANES), jnp.float32)]
        + [pltpu.VMEM((GROUP, total * NY, LANES), jnp.float32)] * 5
        + [pltpu.VMEM((2 * count * planes * NY, LANES), jnp.float32)],
        compiler_params=SMALL,
        cost_estimate=pl.CostEstimate(
            flops=apps * NY * LANES * 50,
            bytes_accessed=(count + 1) * total * cells * 4,
            transcendentals=0,
        ),
        name="filter",
    )(jnp.asarray(z_matrix()), *blocks)

    early = pl.pallas_call(
        functools.partial(near_kernel, planes=planes),
        out_shape=jax.ShapeDtypeStruct((2 * count, LANES), jnp.float32),
        in_specs=[VMEM] * (1 + chips),
        out_specs=VMEM,
        compiler_params=SMALL,
        name="early",
    )(left, *[near[flip] for flip in flips])

    shares = pl.pallas_call(
        functools.partial(far_kernel, planes=planes, flips=flips, total_cells=total * cells),
        out_shape=jax.ShapeDtypeStruct((doms, 2 * count, LANES), jnp.float32),
        in_specs=[VMEM] * (2 + chips),
        out_specs=VMEM,
        compiler_params=SMALL,
        name="late",
    )(left, early, *[far[flip] for flip in flips])
    parts = [shares[0]] + [along_dom(shares[k], k) for k in range(1, doms)]
    return pl.pallas_call(
        sum_kernel,
        out_shape=jax.ShapeDtypeStruct((2, count, orbs * count // doms), jnp.float32),
        in_specs=[VMEM] * doms,
        out_specs=VMEM,
        compiler_params=SMALL,
        name="total",
    )(*parts)


def with_halo(cells, sides, width):
    for axis, dim in sides:
        count = lax.axis_size(axis)
        head = lax.slice_in_dim(cells, 0, width, axis=dim)
        tail = lax.slice_in_dim(cells, cells.shape[dim] - width, cells.shape[dim], axis=dim)
        cells = jnp.concatenate(
            [
                lax.ppermute(tail, axis, [(i, (i + 1) % count) for i in range(count)]),
                cells,
                lax.ppermute(head, axis, [((i + 1) % count, i) for i in range(count)]),
            ],
            axis=dim,
        )
    return cells


def periodic_pad(cube, axis_index):
    extent = cube.shape[axis_index]
    lower = lax.slice_in_dim(cube, extent - RADIUS, extent, axis=axis_index)
    upper = lax.slice_in_dim(cube, 0, RADIUS, axis=axis_index)
    return jnp.concatenate([lower, cube, upper], axis=axis_index)


def stencil_apply(padded, potential, count):
    offset = (potential.shape[0] - count) // 2
    middle = padded[RADIUS : RADIUS + count]
    width = middle.shape[1]
    cube = middle.reshape(count, width, NY, NZ)
    y_padded = periodic_pad(cube, 2)
    z_padded = periodic_pad(cube, 3)
    lap = 3.0 * coeffs[0] * cube
    for step in range(1, 7):
        near = (
            padded[RADIUS + step : RADIUS + step + count]
            + padded[RADIUS - step : RADIUS - step + count]
        )
        near = near.reshape(count, width, NY, NZ)
        near = (
            near
            + y_padded[:, :, RADIUS - step : RADIUS - step + NY]
            + y_padded[:, :, RADIUS + step : RADIUS + step + NY]
        )
        near = (
            near
            + z_padded[:, :, :, RADIUS - step : RADIUS - step + NZ]
            + z_padded[:, :, :, RADIUS + step : RADIUS + step + NZ]
        )
        lap = lap + coeffs[step] * near
    return (-0.5 * lap).reshape(count, width, NY * NZ) + potential[
        offset : offset + count, None, :
    ] * middle


def apply_field(field, potential):
    padded = with_halo(field, (("dom", 0),), RADIUS)
    return stencil_apply(padded, potential, field.shape[0])


def on_device(orbitals, potential):
    planes = orbitals.shape[0]
    current = (apply_field(orbitals, potential) - center_value * orbitals) / half_value
    following = (
        2.0 * (apply_field(current, potential) - center_value * current) / half_value - orbitals
    )
    applied = apply_field(following, potential)
    filt_cells, appl_cells = (
        lax.all_to_all(following, "orb", split_axis=2, concat_axis=1, tiled=True),
        lax.all_to_all(applied, "orb", split_axis=2, concat_axis=1, tiled=True),
    )
    total_cells = planes * lax.axis_size("dom") * orbitals.shape[2]
    correlation = jnp.einsum(
        "xop,xqp->oq",
        filt_cells,
        filt_cells,
        precision=lax.Precision.HIGHEST,
        preferred_element_type=jnp.float32,
    )
    projected = jnp.einsum(
        "xop,xqp->oq",
        filt_cells,
        appl_cells,
        precision=lax.Precision.HIGHEST,
        preferred_element_type=jnp.float32,
    )
    partial_blocks = jnp.stack([correlation, projected]) / total_cells
    row_blocks = lax.psum_scatter(partial_blocks, "orb", scatter_dimension=1, tiled=True)
    return lax.psum_scatter(row_blocks, "dom", scatter_dimension=2, tiled=True)


def fits_gather(mesh):
    doms, orbs = mesh.shape["dom"], mesh.shape["orb"]
    return orbs == 2 * doms and doms == 4


CROSS = 0
RELAYED = True


def solution(mesh):
    gather = fits_gather(mesh)
    return jax.shard_map(
        gathered_device if gather else on_device,
        mesh=mesh,
        in_specs=(P("dom", "orb", None), P("dom", None)),
        out_specs=P(None, "orb", "dom"),
        check_vma=False,
    )
```
